256 devices in a mesh: region: 2 (over core), level: 128 (over z, y, x).
Axes of the slice: x: 4, y: 4, z: 8, core: 2. Of those that a mesh axis runs over, the one named last changes fastest.
Arguments:
- fine_nodes: bfloat16 [327680, 128], P(('region', 'level')), may hold values from -6 to 6
- coarse_nodes: bfloat16 [81920, 128], P(('region', 'level')), may hold values from -6 to 6
- edge_latents: bfloat16 [2097152, 128], P(('region', 'level')), may hold values from -6 to 6
- senders: int32 [2097152], P(('region', 'level')), may hold values from 0 to 1791
- receivers: int32 [2097152], P(('region', 'level')), may hold values from 0 to 1279
- live_blocks: int32 [256], P(('region', 'level')), may hold values from 1 to 64, as said below
- send_list: int32 [131072], P(('region', 'level')), may hold values from 0 to 1279
- parents: int32 [327680], P(('region', 'level')), may hold values from 0 to 40959, as said below
- edge_weight: bfloat16 [384, 128], replicated, may hold values from -0.3125 to 0.3125
- node_weights: bfloat16 [4, 256, 128], replicated, may hold values from -0.375 to 0.375
- out_weights: bfloat16 [5, 128, 128], replicated, may hold values from -0.5 to 0.5
- gains: float32 [5, 128], replicated, may hold values from 0.1 to 1.9
Outputs:
- fine_out: bfloat16 [327680, 128], P(('region', 'level'))
- coarse_out: bfloat16 [81920, 128], P(('region', 'level'))
The draws below stay inside these ranges and needn't reach their ends.
Inputs may be any that keep to these rules, and one draw needn't show every extreme that they name: `senders`: entries below 1280 are the device's own fine nodes; the next 128 come from level index l - 1, the 128 after from level index l + 1, then 128 from each region index in order. `receivers`: own fine nodes of the device. `send_list`: each device's entries hold 128 own local node rows for the device at level index l - 1, then 128 for level index l + 1, then 128 for each region index at the same level index. `parents`: local index into the 40960 coarse nodes of the fine node's region, ordered by level index. A fine node of level index l has its parent in block l (rows l * 320 .. (l + 1) * 320 - 1), in the last 64 rows of block l - 1, or in the first 64 rows of block l + 1; every device with a lower neighbour has a fine node whose parent is row 256 of block l - 1, and every device with an upper neighbour one whose parent is row 63 of block l + 1. The first 128 * live_blocks edge slots of a device are live, the rest padding; in every draw some device has all 64 blocks live.
All inputs are finite; a program needn't handle non-finite values.
Results may differ from the reference program's by a relative error of at most 0.0063.
Values may be sent and summed in bfloat16 or wider, within the bound.
A program may use at most 64 MiB of HBM per device.

```python
import jax
import jax.numpy as jnp
from jax import lax

LAT = 128
NF_DEV = 1280
NC_DEV = 320
BORDER = 64
EBLK = 64
SLOT = 128
NF = 327680
NC = 81920
EDGES = 2097152
N_REGION = 2
N_LEVEL = 128


def draw_live_blocks(key, part):
    key_counts, key_pick = jax.random.split(key)
    device_count = N_REGION * N_LEVEL
    counts = jax.random.randint(key_counts, (device_count,), 1, EBLK + 1)
    chosen = jax.random.randint(key_pick, (), 0, device_count)
    return jnp.where(jnp.arange(device_count) == chosen, EBLK, counts).astype(jnp.int32)


def draw_parents(key, part):
    device_count = N_REGION * N_LEVEL
    key_roll, key_own, key_edge, key_low, key_gap = jax.random.split(jax.random.fold_in(key, 17), 5)
    node = jnp.arange(NF, dtype=jnp.int32)
    device = node // NF_DEV
    local = node % NF_DEV
    level_pos = device % N_LEVEL
    roll = jax.random.randint(key_roll, (NF,), 0, 25)
    own_row = jax.random.randint(key_own, (NF,), 0, NC_DEV)
    edge_row = jax.random.randint(key_edge, (NF,), 0, BORDER)
    pick_low = jax.random.randint(key_low, (device_count,), 0, NF_DEV)
    pick_high = (pick_low + 1 + jax.random.randint(key_gap, (device_count,), 0, NF_DEV - 1)) % NF_DEV
    force_low = local == pick_low[device]
    force_high = local == pick_high[device]
    go_low = (force_low | (roll == 0) & jnp.logical_not(force_high)) & (level_pos > 0)
    go_high = (force_high | (roll == 1) & jnp.logical_not(force_low)) & (level_pos < N_LEVEL - 1) & jnp.logical_not(go_low)
    low_value = (level_pos - 1) * NC_DEV + NC_DEV - BORDER + jnp.where(force_low, 0, edge_row)
    high_value = (level_pos + 1) * NC_DEV + jnp.where(force_high, BORDER - 1, edge_row)
    own_value = level_pos * NC_DEV + own_row
    return jnp.where(go_low, low_value, jnp.where(go_high, high_value, own_value)).astype(jnp.int32)


def set_ends(array, stream_key, smallest, top_value):
    extent = array.shape
    index_at = [jax.random.randint(jax.random.fold_in(stream_key, axis), (), 0, extent[axis]) for axis in range(len(extent))]
    array = array.at[tuple(index_at)].set(smallest)
    longest = extent.index(max(extent))
    index_at[longest] = (index_at[longest] + 1) % extent[longest]
    return array.at[tuple(index_at)].set(top_value)


def steps_of(own_key, shape, cuts, smallest, top_value):
    loudness, own = 1.0, jax.random.fold_in(own_key, 6)
    for axis_at, blocks in cuts:
        steps = jnp.exp(jax.random.uniform(jax.random.fold_in(own, axis_at), (blocks,), jnp.float32, smallest / len(cuts), top_value / len(cuts)))
        loudness = loudness * jnp.repeat(steps, shape[axis_at] // blocks).reshape([-1 if axis == axis_at else 1 for axis in range(len(shape))])
    return loudness


def scatter_about(rng, shape, deviation, most, cuts=(), held_as=jnp.bfloat16):
    loudness = steps_of(rng, shape, cuts, -0.22, 0.18) if cuts else 1.0
    drawn = jax.random.normal(rng, shape, jnp.float32) * deviation * loudness
    return jnp.minimum(jnp.maximum(drawn, -most), most).astype(held_as)


def setup_inputs(seed: int = 0) -> dict:
    splits = jax.random.split(jax.random.key(seed), 13)
    fine_nodes = scatter_about(splits[0], (NF, LAT), 1.0, 6.0, ((0, 256),))
    coarse_nodes = scatter_about(splits[1], (NC, LAT), 1.0, 6.0, ((0, 256),))
    edge_latents = scatter_about(splits[2], (EDGES, LAT), 1.0, 6.0, ((0, 256),))
    senders = set_ends(jax.random.randint(splits[3], (EDGES,), 0, NF_DEV + (2 + N_REGION) * SLOT), jax.random.fold_in(splits[3], 1), 0, (NF_DEV + (2 + N_REGION) * SLOT) - 1).astype(jnp.int32)
    receivers = set_ends(jax.random.randint(splits[4], (EDGES,), 0, NF_DEV), jax.random.fold_in(splits[4], 1), 0, NF_DEV - 1).astype(jnp.int32)
    live_blocks = draw_live_blocks(jax.random.fold_in(splits[12], 71), 0)
    send_list = set_ends(jax.random.randint(splits[6], (N_REGION * N_LEVEL * (2 + N_REGION) * SLOT,), 0, NF_DEV), jax.random.fold_in(splits[6], 1), 0, NF_DEV - 1).astype(jnp.int32)
    parents = draw_parents(jax.random.fold_in(splits[12], 71), 0)
    edge_weight = scatter_about(splits[8], (3 * LAT, LAT), (3 * LAT) ** -0.5, 0.3125)
    node_weights = scatter_about(splits[9], (4, 2 * LAT, LAT), (2 * LAT) ** -0.5, 0.375)
    out_weights = scatter_about(splits[10], (5, LAT, LAT), LAT ** -0.5, 0.5)
    gains = jnp.clip(1.0 + 0.18 * jax.random.normal(splits[11], (5, LAT), jnp.float32), 0.1, 1.9)
    return dict(fine_nodes=fine_nodes, coarse_nodes=coarse_nodes, edge_latents=edge_latents, senders=senders, receivers=receivers, live_blocks=live_blocks, send_list=send_list, parents=parents, edge_weight=edge_weight, node_weights=node_weights, out_weights=out_weights, gains=gains)


norm_eps = 1e-05

def layer_norm(values, gain_row):
    centered = values - lax.optimization_barrier(jnp.mean(values, axis=-1, keepdims=True))
    spread = lax.optimization_barrier(jnp.mean(centered * centered, axis=-1, keepdims=True))
    return centered * lax.rsqrt(spread + norm_eps) * gain_row.astype(jnp.float32)

def perceptron(members, weight_in, weight_out, gain_row):
    lat_width = members[0].shape[1]
    hidden = jnp.zeros((members[0].shape[0], weight_in.shape[1]), jnp.float32)
    for number, member in enumerate(members):
        hidden = hidden + jnp.dot(member, weight_in[number * lat_width:(number + 1) * lat_width], preferred_element_type=jnp.float32)
    active = jax.nn.silu(hidden).astype(jnp.bfloat16)
    return layer_norm(jnp.dot(active, weight_out, preferred_element_type=jnp.float32), gain_row)

def reference(fine_nodes, coarse_nodes, edge_latents, senders, receivers, live_blocks, send_list, parents, edge_weight, node_weights, out_weights, gains):
    device_count = N_REGION * N_LEVEL
    edge_count = EBLK * 128
    list_width = (2 + N_REGION) * SLOT
    device_ids = jnp.arange(device_count, dtype=jnp.int32)
    sends_global = (device_ids[:, None] * NF_DEV + send_list.reshape(device_count, list_width).astype(jnp.int32)).reshape(N_REGION, N_LEVEL, list_width)
    blank = jnp.full((N_REGION, 1, SLOT), NF, jnp.int32)
    from_lower = jnp.concatenate([blank, sends_global[:, :-1, SLOT:2 * SLOT]], 1)
    from_upper = jnp.concatenate([sends_global[:, 1:, :SLOT], blank], 1)
    from_region = sends_global[:, :, 2 * SLOT:].reshape(N_REGION, N_LEVEL, N_REGION, SLOT).transpose(2, 1, 0, 3).reshape(N_REGION, N_LEVEL, N_REGION * SLOT)
    own_index = (device_ids[:, None] * NF_DEV + jnp.arange(NF_DEV, dtype=jnp.int32)[None, :]).reshape(N_REGION, N_LEVEL, NF_DEV)
    extended_index = jnp.concatenate([own_index, from_lower, from_upper, from_region], 2).reshape(device_count, NF_DEV + list_width).astype(jnp.int32)
    padded_fine = jnp.concatenate([fine_nodes, jnp.zeros((1, LAT), jnp.bfloat16)], 0)
    coarse_base = (device_ids // N_LEVEL * (N_LEVEL * NC_DEV)).astype(jnp.int32)
    node_blocks = fine_nodes.reshape(device_count, NF_DEV, LAT)
    parent_blocks = parents.reshape(device_count, NF_DEV).astype(jnp.int32)

    def fine_section(inputs):
        own_nodes, latents, sender_ids, receiver_ids, ext_index, live_count, parent_rows, coarse_start = inputs
        sources = padded_fine[ext_index[sender_ids]]
        targets = own_nodes[receiver_ids]
        message = perceptron((latents, sources, targets), edge_weight, out_weights[0], gains[0])
        updated = (latents.astype(jnp.float32) + message).astype(jnp.bfloat16)
        live_mask = jnp.arange(edge_count) < live_count * 128
        contrib = jnp.where(live_mask[:, None], updated.astype(jnp.float32), 0.0)
        aggregated = jax.ops.segment_sum(contrib, receiver_ids, num_segments=NF_DEV).astype(jnp.bfloat16)
        fine_mid = (own_nodes.astype(jnp.float32) + perceptron((own_nodes, aggregated), node_weights[0], out_weights[1], gains[1])).astype(jnp.bfloat16)
        parent_latents = coarse_nodes[coarse_start + parent_rows]
        upward = perceptron((fine_mid, parent_latents), node_weights[1], out_weights[2], gains[2])
        return (fine_mid, upward)
    fine_mid, upward = lax.map(fine_section, (node_blocks, edge_latents.reshape(device_count, edge_count, LAT), senders.reshape(device_count, edge_count), receivers.reshape(device_count, edge_count), extended_index, live_blocks, parent_blocks, coarse_base))
    parent_global = (coarse_base[:, None] + parent_blocks).reshape(-1)
    up_sum = jax.ops.segment_sum(upward.reshape(-1, LAT), parent_global, num_segments=NC_DEV * device_count).astype(jnp.bfloat16)
    coarse_out = (coarse_nodes.astype(jnp.float32) + perceptron((coarse_nodes, up_sum), node_weights[2], out_weights[3], gains[3])).astype(jnp.bfloat16)

    def down_section(inputs):
        mid_nodes, parent_rows, coarse_start = inputs
        parent_latents = coarse_out[coarse_start + parent_rows]
        return (mid_nodes.astype(jnp.float32) + perceptron((mid_nodes, parent_latents), node_weights[3], out_weights[4], gains[4])).astype(jnp.bfloat16)
    fine_out = lax.map(down_section, (fine_mid, parent_blocks, coarse_base))
    return (fine_out.reshape(device_count * NF_DEV, LAT), coarse_out)
```

```python
import functools

import jax
import jax.numpy as jnp
from jax import lax
from jax.experimental import pallas as pl
from jax.experimental.pallas import tpu as pltpu
from jax.sharding import PartitionSpec as P

MESH = pl.DeviceIdType.MESH
F32 = jnp.float32
BF16 = jnp.bfloat16
LAT = 128
BORDER = 64
SLOT = 128
norm_eps = 1e-05
group_edges = 1024
TILE = 256


def dot(a, b, ca=1, cb=0):
    return lax.dot_general(a, b, (((ca,), (cb,)), ((), ())), preferred_element_type=F32)


def silu(v):
    h = 0.5 * v
    return (h * jnp.tanh(h) + h).astype(BF16)


def norm_rows(o):
    c = o - jnp.mean(o, axis=1, keepdims=True)
    return c * lax.rsqrt(jnp.mean(c * c, axis=1, keepdims=True) + norm_eps)


def norm_columns(o):
    c = o - jnp.mean(o, axis=0, keepdims=True)
    return c * lax.rsqrt(jnp.mean(c * c, axis=0, keepdims=True) + norm_eps)


def one_hot_columns(low, rows):
    shape = (rows, low.shape[1])
    ids = lax.broadcasted_iota(jnp.int32, shape, 0).astype(BF16)
    return jnp.where(ids == jnp.broadcast_to(low, shape), jnp.ones((), BF16), jnp.zeros((), BF16))


def split(x):
    high = x.astype(BF16)
    return jnp.concatenate([high, (x - high.astype(F32)).astype(BF16)], axis=1)


def pick(products, high, count):
    x = products[:LAT]
    for g in range(1, count):
        x = jnp.where(high == g, products[g * LAT : (g + 1) * LAT], x)
    return x


def low_high(ids):
    return (ids & (TILE - 1)).astype(F32).astype(BF16), ids >> 8


def kernel(
    levels,
    fine,
    coarse,
    latents,
    senders,
    receivers,
    live,
    send_list,
    parents,
    edge_w,
    node_w,
    out_w,
    gains,
    fine_out,
    coarse_out,
    lat_v,
    sender_t,
    receiver_t,
    outgoing,
    arrived,
    cext,
    par_rows,
    par_cols,
    up_pre,
    down_pre,
    mid,
    sums_out,
    sums_in,
    acc,
    weights_t,
    gain_t,
    lat_sem,
    send_sem,
    recv_sem,
):
    r, l = lax.axis_index("region"), lax.axis_index("level")
    nodes, blocks = fine.shape[0], coarse.shape[0]
    ext = blocks + 2 * BORDER
    groups = nodes // TILE
    slots = arrived.shape[0]
    edges = latents.shape[0]
    has_lower, has_upper = l > 0, l < levels - 1
    lower, upper, peer = (r, l - 1), (r, l + 1), (1 - r, l)

    load = pltpu.make_async_copy(latents, lat_v, lat_sem)
    load.start()

    barrier = pltpu.get_barrier_semaphore()
    pl.semaphore_signal(barrier, inc=1, device_id=peer, device_id_type=MESH)

    @pl.when(has_lower)
    def _():
        pl.semaphore_signal(barrier, inc=1, device_id=lower, device_id_type=MESH)

    @pl.when(has_upper)
    def _():
        pl.semaphore_signal(barrier, inc=1, device_id=upper, device_id_type=MESH)

    def remote(kind, src, dst, device):
        return pltpu.make_async_remote_copy(
            src_ref=src,
            dst_ref=dst,
            send_sem=send_sem.at[kind],
            recv_sem=recv_sem.at[kind],
            device_id=device,
            device_id_type=MESH,
        )

    halo_down = remote(0, outgoing.at[0], arrived.at[1], lower)
    halo_up = remote(1, outgoing.at[1], arrived.at[0], upper)
    halo_peer = remote(2, outgoing.at[3 - r], arrived.at[2 + r], peer)
    coarse_down = remote(
        3, coarse.at[pl.ds(0, BORDER)], cext.at[pl.ds(BORDER + blocks, BORDER)], lower
    )
    coarse_up = remote(
        4, coarse.at[pl.ds(blocks - BORDER, BORDER)], cext.at[pl.ds(0, BORDER)], upper
    )
    sums_down = remote(5, sums_out.at[pl.ds(0, 2 * BORDER)], sums_in.at[1], lower)
    sums_up = remote(6, sums_out.at[pl.ds(blocks, 2 * BORDER)], sums_in.at[0], upper)

    w_sender = edge_w[LAT : 2 * LAT, :].T
    w_receiver = edge_w[2 * LAT :, :].T
    w_both = jnp.concatenate([w_sender, w_receiver], axis=0)
    for g in range(groups):
        both = dot(w_both, fine[g * TILE : (g + 1) * TILE, :], 1, 1).astype(BF16)
        sender_t[g * LAT : (g + 1) * LAT, :] = both[:LAT]
        receiver_t[g * LAT : (g + 1) * LAT, :] = both[LAT:]

    sends = jnp.concatenate([send_list[j : j + 1, :] for j in range(slots)], axis=1)
    low, high = low_high(sends)
    picked = pick(
        dot(sender_t[: groups * LAT, :], one_hot_columns(low, TILE)), high, groups
    ).astype(BF16)
    for j in range(slots):
        outgoing[j] = picked[:, j * SLOT : (j + 1) * SLOT]

    pl.semaphore_wait(barrier, 1 + has_lower.astype(jnp.int32) + has_upper.astype(jnp.int32))
    halo_peer.start()

    @pl.when(has_lower)
    def _():
        halo_down.start()
        coarse_down.start()

    @pl.when(has_upper)
    def _():
        halo_up.start()
        coarse_up.start()

    arrived[2 + r] = outgoing[2 + r]
    cext[BORDER : BORDER + blocks, :] = coarse[...]
    cext[ext:, :] = jnp.zeros((cext.shape[0] - ext, LAT), BF16)

    @pl.when(jnp.logical_not(has_lower))
    def _():
        arrived[0] = jnp.zeros((LAT, SLOT), BF16)
        cext[:BORDER, :] = jnp.zeros((BORDER, LAT), BF16)
        sums_in[0] = jnp.zeros((2 * BORDER, LAT), BF16)

    @pl.when(jnp.logical_not(has_upper))
    def _():
        arrived[1] = jnp.zeros((LAT, SLOT), BF16)
        cext[BORDER + blocks : ext, :] = jnp.zeros((BORDER, LAT), BF16)
        sums_in[1] = jnp.zeros((2 * BORDER, LAT), BF16)

    weights_t[:LAT, :] = edge_w[:LAT, :].T
    eye = lax.broadcasted_iota(jnp.int32, (LAT, LAT), 0) == lax.broadcasted_iota(
        jnp.int32, (LAT, LAT), 1
    )
    weights_t[LAT : 2 * LAT, :] = jnp.where(eye, 1.0, 0.0).astype(BF16)
    weights_t[2 * LAT :, :] = out_w[0].T
    gain_t[...] = jnp.broadcast_to(gains[0:1, :], (LAT, LAT)).T
    acc[...] = jnp.zeros_like(acc)
    offset = BORDER - l * blocks
    width = par_cols.shape[0]
    for j in range(nodes // LAT):
        place = (parents[j : j + 1, :] + offset).astype(F32)
        wide = jnp.broadcast_to(place, (width, LAT))
        ids = lax.broadcasted_iota(jnp.int32, (width, LAT), 0).astype(F32)
        par_cols[:, j * LAT : (j + 1) * LAT] = jnp.where(ids == wide, 1.0, 0.0).astype(BF16)
        column = jnp.broadcast_to(place, (LAT, LAT)).T
        ids = lax.broadcasted_iota(jnp.int32, (LAT, LAT), 1).astype(F32)
        for k in range(width // LAT):
            par_rows[j * LAT : (j + 1) * LAT, k * LAT : (k + 1) * LAT] = jnp.where(
                ids + float(k * LAT) == column, 1.0, 0.0
            ).astype(BF16)

    halo_peer.wait()

    @pl.when(has_lower)
    def _():
        halo_down.wait_send()
        halo_up.wait_recv()
        coarse_down.wait_send()
        coarse_up.wait_recv()

    @pl.when(has_upper)
    def _():
        halo_up.wait_send()
        halo_down.wait_recv()
        coarse_up.wait_send()
        coarse_down.wait_recv()

    for j in range(slots // 2):
        g = groups + j
        sender_t[g * LAT : (g + 1) * LAT, :] = jnp.concatenate(
            [arrived[2 * j], arrived[2 * j + 1]], axis=1
        )

    up_table = split(dot(cext[...], node_w[1, LAT:, :]))
    for g in range(groups):
        rows = slice(g * TILE, (g + 1) * TILE)
        found = dot(par_rows[rows, :], up_table)
        up_pre[rows, :] = found[:, :LAT] + found[:, LAT:]

    load.wait()
    sub = group_edges // LAT

    def add_group(b, carry):
        def row(ref):
            return jnp.concatenate([ref[pl.ds(b * sub + j, 1), :] for j in range(sub)], axis=1)

        s_low, s_high = low_high(row(senders))
        r_low, r_high = low_high(row(receivers))
        lat = lat_v[pl.ds(pl.multiple_of(b * group_edges, group_edges), group_edges), :]
        first = dot(weights_t[: 2 * LAT, :], lat, 1, 1)
        r_hot = one_hot_columns(r_low, TILE)
        hidden = first[:LAT] + pick(dot(sender_t[...], one_hot_columns(s_low, TILE)), s_high, 7)
        hidden = hidden + pick(dot(receiver_t[...], r_hot), r_high, groups)
        message = norm_columns(dot(weights_t[2 * LAT :, :], silu(hidden)))
        updated = (first[LAT:] + message * jnp.concatenate([gain_t[...]] * sub, axis=1)).astype(BF16)
        position = b * group_edges + lax.broadcasted_iota(jnp.int32, (1, group_edges), 1)
        target = jnp.where(position < live[0] * 128, r_high, groups)
        spread = jnp.concatenate(
            [
                updated
                * jnp.broadcast_to(jnp.where(target == g, 1.0, 0.0).astype(BF16), updated.shape)
                for g in range(groups)
            ],
            axis=0,
        )
        acc[...] += dot(spread, r_hot, 1, 1)
        return carry

    lax.fori_loop(0, edges // group_edges, add_group, 0)

    sums = jnp.zeros((width, 2 * LAT), F32)
    for g in range(groups):
        rows = slice(g * TILE, (g + 1) * TILE)
        own = fine[rows, :]
        agg = acc[g * LAT : (g + 1) * LAT, :].T.astype(BF16)
        hidden = dot(jnp.concatenate([own, agg], axis=1), node_w[0])
        new = norm_rows(dot(silu(hidden), out_w[1])) * gains[1:2, :]
        new = (own.astype(F32) + new).astype(BF16)
        mid[rows, :] = new
        hidden = dot(new, node_w[1, :LAT, :]) + up_pre[rows, :]
        upward = norm_rows(dot(silu(hidden), out_w[2])) * gains[2:3, :]
        sums = sums + dot(par_cols[:, rows], split(upward))
    sums = sums[:, :LAT] + sums[:, LAT:]
    sums_out[...] = sums[:ext].astype(BF16)

    @pl.when(has_lower)
    def _():
        sums_down.start()

    @pl.when(has_upper)
    def _():
        sums_up.start()

    for g in range(groups):
        rows = slice(g * TILE, (g + 1) * TILE)
        down_pre[rows, :] = dot(mid[rows, :], node_w[3, :LAT, :])

    @pl.when(has_lower)
    def _():
        sums_down.wait_send()
        sums_up.wait_recv()

    @pl.when(has_upper)
    def _():
        sums_up.wait_send()
        sums_down.wait_recv()

    total = jnp.concatenate(
        [
            sums[: 2 * BORDER] + sums_in[0].astype(F32),
            sums[2 * BORDER : blocks],
            sums[blocks:ext] + sums_in[1].astype(F32),
        ],
        axis=0,
    ).astype(BF16)
    base = cext[:ext, :]
    hidden = dot(jnp.concatenate([base, total], axis=1), node_w[2])
    new = norm_rows(dot(silu(hidden), out_w[3])) * gains[3:4, :]
    new = (base.astype(F32) + new).astype(BF16)
    coarse_out[...] = new[BORDER : BORDER + blocks]
    down_table = split(dot(new, node_w[3, LAT:, :]))
    for g in range(groups):
        rows = slice(g * TILE, (g + 1) * TILE)
        found = dot(par_rows[rows, :ext], down_table)
        hidden = down_pre[rows, :] + found[:, :LAT] + found[:, LAT:]
        new = norm_rows(dot(silu(hidden), out_w[4])) * gains[4:5, :]
        fine_out[rows, :] = (mid[rows, :].astype(F32) + new).astype(BF16)


def body(
    levels,
    fine_nodes,
    coarse_nodes,
    edge_latents,
    senders,
    receivers,
    live_blocks,
    send_list,
    parents,
    edge_weight,
    node_weights,
    out_weights,
    gains,
):
    nodes, blocks, edges = fine_nodes.shape[0], coarse_nodes.shape[0], edge_latents.shape[0]
    groups, slots = nodes // TILE, send_list.shape[0] // SLOT
    ext = blocks + 2 * BORDER
    width = (ext + LAT - 1) // LAT * LAT
    vmem = pl.BlockSpec(memory_space=pltpu.VMEM)
    specs = [vmem] * 12
    specs[2] = pl.BlockSpec(memory_space=pl.ANY)
    specs[5] = pl.BlockSpec(memory_space=pltpu.SMEM)
    return tuple(
        pl.pallas_call(
            functools.partial(kernel, levels),
            out_shape=(
                jax.ShapeDtypeStruct(fine_nodes.shape, BF16),
                jax.ShapeDtypeStruct(coarse_nodes.shape, BF16),
            ),
            in_specs=specs,
            out_specs=(vmem, vmem),
            scratch_shapes=[
                pltpu.VMEM((edges, LAT), BF16),
                pltpu.VMEM(((groups + slots // 2) * LAT, TILE), BF16),
                pltpu.VMEM((groups * LAT, TILE), BF16),
                pltpu.VMEM((slots, LAT, SLOT), BF16),
                pltpu.VMEM((slots, LAT, SLOT), BF16),
                pltpu.VMEM((width, LAT), BF16),
                pltpu.VMEM((nodes, width), BF16),
                pltpu.VMEM((width, nodes), BF16),
                pltpu.VMEM((nodes, LAT), F32),
                pltpu.VMEM((nodes, LAT), F32),
                pltpu.VMEM((nodes, LAT), BF16),
                pltpu.VMEM((ext, LAT), BF16),
                pltpu.VMEM((2, 2 * BORDER, LAT), BF16),
                pltpu.VMEM((groups * LAT, TILE), F32),
                pltpu.VMEM((3 * LAT, LAT), BF16),
                pltpu.VMEM((LAT, LAT), F32),
                pltpu.SemaphoreType.DMA,
                pltpu.SemaphoreType.DMA((7,)),
                pltpu.SemaphoreType.DMA((7,)),
            ],
            compiler_params=pltpu.CompilerParams(collective_id=0, has_side_effects=True),
            name="graph_step",
        )(
            fine_nodes,
            coarse_nodes,
            edge_latents,
            senders.reshape(-1, LAT),
            receivers.reshape(-1, LAT),
            live_blocks,
            send_list.reshape(-1, SLOT),
            parents.reshape(-1, LAT),
            edge_weight,
            node_weights,
            out_weights,
            gains,
        )
    )


def solution(mesh):
    both = ("region", "level")
    in_specs = (
        P(both, None),
        P(both, None),
        P(both, None),
        P(both),
        P(both),
        P(both),
        P(both),
        P(both),
        P(),
        P(),
        P(),
        P(),
    )
    return jax.shard_map(
        functools.partial(body, mesh.shape["level"]),
        mesh=mesh,
        in_specs=in_specs,
        out_specs=(P(both, None), P(both, None)),
        check_vma=False,
    )
```

```python
import functools

import jax
import jax.numpy as jnp
from jax import lax
from jax.experimental import pallas as pl
from jax.experimental.pallas import tpu as pltpu
from jax.sharding import PartitionSpec as P

MESH = pl.DeviceIdType.MESH
F32 = jnp.float32
BF16 = jnp.bfloat16
I32 = jnp.int32
LAT = 128
HALF = LAT // 2
BORDER = 64
EDGE_ROWS = 4 * BORDER
SLOT = 128
norm_eps = 1e-05
group_edges = 1024
sub = group_edges // LAT
TILE = 256
ahead = 2
lane_tiles = 4
top = 16380.0


def dot(a, b, ca=1, cb=0):
    return lax.dot_general(a, b, (((ca,), (cb,)), ((), ())), preferred_element_type=F32)


def half_silu(h):
    return (h * jnp.tanh(h) + h).astype(BF16)


def scale_rows(c):
    return c * lax.rsqrt(jnp.mean(c * c, axis=1, keepdims=True) + norm_eps)


def hot_columns(ids, rows):
    low, high = (ids & (TILE - 1)).astype(F32), ids >> 8
    shape = (TILE, ids.shape[1])
    place = lax.broadcasted_iota(I32, shape, 0).astype(BF16)
    parts = []
    for g in range(rows // TILE):
        mine = jnp.where(high == g, low, -1.0).astype(BF16)
        parts.append(
            jnp.where(place == jnp.broadcast_to(mine, shape), jnp.ones((), BF16), jnp.zeros((), BF16))
        )
    return jnp.concatenate(parts, axis=0)


def split(x, axis):
    high = x.astype(BF16)
    return jnp.concatenate([high, (x - high.astype(F32)).astype(BF16)], axis=axis)


def centered(w):
    wide = w.astype(F32)
    return split(wide - jnp.mean(wide, axis=1, keepdims=True), 0)


def twice(x, axis=1):
    return jnp.concatenate([x, x], axis=axis)


def kernel(
    levels,
    fine_h,
    coarse_h,
    latents_h,
    senders_h,
    receivers_h,
    live_h,
    send_list_h,
    parents_h,
    edge_w_h,
    node_w_h,
    out_w_h,
    gains_h,
    mid,
    down_pre,
    par_edge,
    base_edge,
    total_edge,
    new_inner,
    late_w,
    late_out,
    late_gain,
    fine,
    coarse,
    latents,
    senders,
    receivers,
    live,
    send_list,
    parents,
    edge_w,
    node_w,
    out_w,
    gains,
    table,
    full,
    sender_q,
    receiver_q,
    packed,
    acts,
    outgoing,
    arrived,
    cext,
    par_inner,
    par_cols,
    up_pre,
    sums_out,
    sums_in,
    acc,
    first_t,
    second_t,
    gain_t,
    scale_t,
    load_sem,
    send_sem,
    recv_sem,
):
    r, l = lax.axis_index("region"), lax.axis_index("level")
    nodes, blocks = fine.shape[0], coarse.shape[0]
    inner = blocks - 2 * BORDER
    ext = blocks + 2 * BORDER
    groups = nodes // TILE
    slots = arrived.shape[0]
    edge_blocks = latents.shape[0] // group_edges
    has_lower, has_upper = l > 0, l < levels - 1
    lower, upper, peer = (r, l - 1), (r, l + 1), (1 - r, l)

    barrier = pltpu.get_barrier_semaphore()
    pl.semaphore_signal(barrier, inc=1, device_id=peer, device_id_type=MESH)

    @pl.when(has_lower)
    def _():
        pl.semaphore_signal(barrier, inc=1, device_id=lower, device_id_type=MESH)

    @pl.when(has_upper)
    def _():
        pl.semaphore_signal(barrier, inc=1, device_id=upper, device_id_type=MESH)

    pairs = [
        (edge_w_h, edge_w),
        (fine_h, fine),
        (send_list_h, send_list),
        (coarse_h, coarse),
        (receivers_h, receivers),
        (senders_h, senders),
        (parents_h, parents),
        (latents_h, latents),
        (out_w_h, out_w),
        (gains_h, gains),
        (node_w_h, node_w),
        (live_h, live),
    ]
    loads = [pltpu.make_async_copy(s, d, load_sem.at[k]) for k, (s, d) in enumerate(pairs)]
    for load in loads:
        load.start()

    def remote(kind, src, dst, device):
        return pltpu.make_async_remote_copy(
            src_ref=src,
            dst_ref=dst,
            send_sem=send_sem.at[kind],
            recv_sem=recv_sem.at[kind],
            device_id=device,
            device_id_type=MESH,
        )

    halo_down = remote(0, outgoing.at[0], arrived.at[1], lower)
    halo_up = remote(1, outgoing.at[1], arrived.at[0], upper)
    halo_peer = remote(2, outgoing.at[3 - r], arrived.at[2 + r], peer)
    coarse_down = remote(3, coarse.at[pl.ds(0, BORDER)], cext.at[pl.ds(3 * BORDER, BORDER)], lower)
    coarse_up = remote(4, coarse.at[pl.ds(blocks - BORDER, BORDER)], cext.at[pl.ds(0, BORDER)], upper)
    sums_down = remote(5, sums_out.at[0], sums_in.at[1], lower)
    sums_up = remote(6, sums_out.at[1], sums_in.at[0], upper)

    loads[0].wait()
    w_both = jnp.concatenate(
        [
            (edge_w[LAT : 2 * LAT, :].astype(F32) * 0.5).T.astype(BF16),
            (edge_w[2 * LAT :, :].astype(F32) * 0.5).T.astype(BF16),
        ],
        axis=0,
    )
    loads[1].wait()
    for g in range(groups):
        both = dot(w_both, fine[g * TILE : (g + 1) * TILE, :], 1, 1)
        full[:, g * TILE : (g + 1) * TILE] = both
        table[:, g * TILE : (g + 1) * TILE] = both[:LAT].astype(BF16)

    loads[2].wait()
    sends = jnp.concatenate([send_list[j : j + 1, :] for j in range(slots)], axis=1)
    picked = dot(table[:, :nodes], hot_columns(sends, nodes)).astype(BF16)
    for j in range(slots):
        outgoing[j] = picked[:, j * SLOT : (j + 1) * SLOT]
    loads[3].wait()

    pl.semaphore_wait(barrier, 1 + has_lower.astype(I32) + has_upper.astype(I32))

    @pl.when(has_lower)
    def _():
        halo_down.start()

    @pl.when(has_upper)
    def _():
        halo_up.start()

    halo_peer.start()

    @pl.when(has_lower)
    def _():
        coarse_down.start()

    @pl.when(has_upper)
    def _():
        coarse_up.start()

    arrived[2 + r] = outgoing[2 + r]
    cext[BORDER : 2 * BORDER, :] = coarse[:BORDER, :]
    cext[2 * BORDER : 3 * BORDER, :] = coarse[blocks - BORDER :, :]
    cext[EDGE_ROWS : EDGE_ROWS + inner, :] = coarse[BORDER : blocks - BORDER, :]
    cext[EDGE_ROWS + inner :, :] = jnp.zeros((cext.shape[0] - EDGE_ROWS - inner, LAT), BF16)

    @pl.when(jnp.logical_not(has_lower))
    def _():
        arrived[0] = jnp.zeros((LAT, SLOT), BF16)
        cext[:BORDER, :] = jnp.zeros((BORDER, LAT), BF16)
        sums_in[0] = jnp.zeros((2 * BORDER, LAT), BF16)

    @pl.when(jnp.logical_not(has_upper))
    def _():
        arrived[1] = jnp.zeros((LAT, SLOT), BF16)
        cext[3 * BORDER : 4 * BORDER, :] = jnp.zeros((BORDER, LAT), BF16)
        sums_in[1] = jnp.zeros((2 * BORDER, LAT), BF16)

    most = jnp.max(jnp.abs(full[...]), axis=1, keepdims=True)
    most = jnp.maximum(jnp.maximum(most[:LAT], most[LAT:]), 1e-30)
    step = most * (1.0 / top)
    scale_t[...] = jnp.broadcast_to(step * (1.0 / 65536.0), (LAT, LAT))
    inverse = top / most

    def pack(start, count, target):
        for t in range(count):
            cols = slice(t * LAT, (t + 1) * LAT)
            q = full[start : start + LAT, cols] * inverse
            low = jnp.round(q[HALF:])
            high = jnp.round(q[:HALF] - low * (1.0 / 65536.0))
            target[:, cols] = high.astype(I32) * 65536 + low.astype(I32)

    pack(0, lane_tiles, sender_q)
    pack(LAT, nodes // LAT, receiver_q)

    def gather(b):
        for j in range(sub):

            def look_up(ids, target, x, count):
                low = jnp.broadcast_to(ids & (LAT - 1), (HALF, LAT))
                high = jnp.broadcast_to(ids >> 7, (HALF, LAT))
                for t in range(count):
                    found = jnp.take_along_axis(target[:, t * LAT : (t + 1) * LAT], low, axis=1)
                    x = found if x is None else jnp.where(high == t, found, x)
                return x

            s, t = senders[pl.ds(b * sub + j, 1), :], receivers[pl.ds(b * sub + j, 1), :]
            total = look_up(t, receiver_q, None, nodes // LAT)
            total = total + look_up(s, sender_q, jnp.zeros((HALF, LAT), I32), lane_tiles)
            packed[b, :, j * LAT : (j + 1) * LAT] = total

    loads[4].wait()
    loads[5].wait()

    def gather_step(b, carry):
        gather(b)
        return carry

    lax.fori_loop(0, ahead, gather_step, 0)

    loads[6].wait()
    offset = BORDER - l * blocks
    for j in range(nodes // LAT):
        p = parents[j : j + 1, :] + offset
        p = jnp.where(
            p < 2 * BORDER, p, jnp.where(p < 2 * BORDER + inner, p + 2 * BORDER, p - inner)
        )
        par_cols[:, j * LAT : (j + 1) * LAT] = hot_columns(p, par_cols.shape[0])
        column = jnp.broadcast_to(p.astype(F32), (LAT, LAT)).T
        ids = lax.broadcasted_iota(I32, (LAT, LAT), 1).astype(F32)
        rows = slice(j * LAT, (j + 1) * LAT)
        for k in range(2):
            cols = slice(k * LAT, (k + 1) * LAT)
            par_edge[rows, cols] = jnp.where(ids + float(k * LAT) == column, 1.0, 0.0).astype(BF16)
            par_inner[rows, cols] = jnp.where(
                ids + float(EDGE_ROWS + k * LAT) == column, 1.0, 0.0
            ).astype(BF16)

    for k in range(7, 12):
        loads[k].wait()
    first_t[:LAT, :] = (edge_w[:LAT, :].astype(F32) * 0.5).T.astype(BF16)
    eye = lax.broadcasted_iota(I32, (LAT, LAT), 0) == lax.broadcasted_iota(I32, (LAT, LAT), 1)
    first_t[LAT:, :] = jnp.where(eye, 1.0, 0.0).astype(BF16)
    wide = out_w[0].astype(F32).T
    second_t[...] = split(wide - jnp.mean(wide, axis=0, keepdims=True), 1)
    gain_t[...] = jnp.broadcast_to(gains[0:1, :], (LAT, LAT)).T
    acc[...] = jnp.zeros_like(acc)
    late_w[...] = node_w[2:4]
    late_out[0] = centered(out_w[3])
    late_out[1] = centered(out_w[4])
    late_gain[...] = gains[...]

    halo_peer.wait()

    @pl.when(has_lower)
    def _():
        halo_down.wait_send()
        halo_up.wait_recv()
        coarse_down.wait_send()
        coarse_up.wait_recv()

    @pl.when(has_upper)
    def _():
        halo_up.wait_send()
        halo_down.wait_recv()
        coarse_up.wait_send()
        coarse_down.wait_recv()

    for j in range(slots):
        table[:, nodes + j * SLOT : nodes + (j + 1) * SLOT] = arrived[j]

    gain_all = jnp.concatenate([gain_t[...]] * sub, axis=1)
    scale_all = jnp.concatenate([scale_t[...]] * sub, axis=1)
    skip = lane_tiles * LAT
    listed = table.shape[1]

    def row(ref, b):
        return jnp.concatenate([ref[pl.ds(b * sub + j, 1), :] for j in range(sub)], axis=1)

    def block(b):
        return latents[pl.ds(pl.multiple_of(b * group_edges, group_edges), group_edges), :]

    def hidden_layer(b):
        h = dot(first_t[:LAT, :], block(b), 1, 1)
        h = h + dot(table[:, skip:], hot_columns(row(senders, b) - skip, listed - skip))
        own = packed[b]
        own = jnp.concatenate([own.astype(F32), (own << 16).astype(F32)], axis=0)
        acts[b] = half_silu(h + own * scale_all)

    def add_edges(b):
        lat = dot(first_t[LAT:, :], block(b), 1, 1)
        c = dot(second_t[...], twice(acts[b], 0))
        spread = lax.rsqrt(jnp.mean(c * c, axis=0, keepdims=True) + norm_eps)
        updated = (lat + c * spread * gain_all).astype(BF16)
        ids = row(receivers, b)
        position = b * group_edges + lax.broadcasted_iota(I32, (1, group_edges), 1)
        target = jnp.where(position < live[0] * 128, ids >> 8, groups)
        masked = jnp.concatenate(
            [
                updated
                * jnp.broadcast_to(jnp.where(target == g, 1.0, 0.0).astype(BF16), updated.shape)
                for g in range(groups)
            ],
            axis=0,
        )
        acc[...] += dot(masked, hot_columns(ids & (TILE - 1), TILE), 1, 1)

    hidden_layer(0)

    def full_step(b, carry):
        add_edges(b)
        hidden_layer(b + 1)
        gather(b + ahead)
        return carry

    def last_step(b, carry):
        add_edges(b)
        hidden_layer(b + 1)
        return carry

    lax.fori_loop(0, edge_blocks - ahead, full_step, 0)
    lax.fori_loop(edge_blocks - ahead, edge_blocks - 1, last_step, 0)
    add_edges(edge_blocks - 1)

    up_table = split(dot(cext[...], node_w[1, LAT:, :]), 1)
    for g in range(groups):
        rows = slice(g * TILE, (g + 1) * TILE)
        found = dot(par_edge[rows, :], up_table[:TILE]) + dot(par_inner[rows, :], up_table[TILE:])
        up_pre[rows, :] = found[:, :LAT] + found[:, LAT:]

    fine_out_w, up_out_w = centered(out_w[1]), centered(out_w[2])
    sums = jnp.zeros((cext.shape[0], 2 * LAT), F32)
    for g in range(groups):
        rows = slice(g * TILE, (g + 1) * TILE)
        own = fine[rows, :]
        agg = acc[g * LAT : (g + 1) * LAT, :].T.astype(BF16)
        h = dot(jnp.concatenate([own, agg], axis=1), node_w[0])
        new = scale_rows(dot(twice(half_silu(0.5 * h)), fine_out_w)) * gains[1:2, :]
        new = (own.astype(F32) + new).astype(BF16)
        mid[rows, :] = new
        h = dot(new, node_w[1, :LAT, :]) + up_pre[rows, :]
        upward = scale_rows(dot(twice(half_silu(0.5 * h)), up_out_w)) * gains[2:3, :]
        sums = sums + dot(par_cols[:, rows], split(upward, 1))
    sums = sums[:, :LAT] + sums[:, LAT:]
    sums_out[0] = sums[: 2 * BORDER].astype(BF16)
    sums_out[1] = sums[2 * BORDER : EDGE_ROWS].astype(BF16)

    @pl.when(has_lower)
    def _():
        sums_down.start()

    @pl.when(has_upper)
    def _():
        sums_up.start()

    base = cext[EDGE_ROWS:, :]
    h = dot(jnp.concatenate([base, sums[EDGE_ROWS:].astype(BF16)], axis=1), node_w[2])
    new = scale_rows(dot(twice(half_silu(0.5 * h)), late_out[0])) * gains[3:4, :]
    new = (base.astype(F32) + new).astype(BF16)
    new_inner[...] = new[:inner]
    inner_table = split(dot(new, node_w[3, LAT:, :]), 1)
    for g in range(groups):
        rows = slice(g * TILE, (g + 1) * TILE)
        found = dot(par_inner[rows, :], inner_table)
        down_pre[rows, :] = dot(mid[rows, :], node_w[3, :LAT, :]) + (found[:, :LAT] + found[:, LAT:])
    base_edge[...] = cext[:EDGE_ROWS, :]

    @pl.when(has_lower)
    def _():
        sums_down.wait_send()
        sums_up.wait_recv()

    @pl.when(has_upper)
    def _():
        sums_up.wait_send()
        sums_down.wait_recv()

    total_edge[: 2 * BORDER, :] = (sums[: 2 * BORDER] + sums_in[0].astype(F32)).astype(BF16)
    total_edge[2 * BORDER :, :] = (sums[2 * BORDER : EDGE_ROWS] + sums_in[1].astype(F32)).astype(BF16)


def finish(
    mid,
    down_pre,
    par_edge,
    base_edge,
    total_edge,
    new_inner,
    late_w,
    late_out,
    late_gain,
    fine_out,
    coarse_out,
    fine_v,
    coarse_v,
    sem,
):
    nodes, blocks = fine_v.shape[0], coarse_v.shape[0]
    base = base_edge[...]
    h = dot(jnp.concatenate([base, total_edge[...]], axis=1), late_w[0])
    new = scale_rows(dot(twice(half_silu(0.5 * h)), late_out[0])) * late_gain[3:4, :]
    new = (base.astype(F32) + new).astype(BF16)
    coarse_v[:BORDER, :] = new[BORDER : 2 * BORDER]
    coarse_v[blocks - BORDER :, :] = new[2 * BORDER : 3 * BORDER]
    coarse_v[BORDER : blocks - BORDER, :] = new_inner[...]
    copies = [pltpu.make_async_copy(coarse_v, coarse_out, sem.at[nodes // TILE])]
    copies[0].start()
    edge_table = split(dot(new, late_w[1, LAT:, :]), 1)
    for g in range(nodes // TILE):
        rows = slice(g * TILE, (g + 1) * TILE)
        found = dot(par_edge[rows, :], edge_table)
        h = down_pre[rows, :] + (found[:, :LAT] + found[:, LAT:])
        new = scale_rows(dot(twice(half_silu(0.5 * h)), late_out[1])) * late_gain[4:5, :]
        fine_v[rows, :] = (mid[rows, :].astype(F32) + new).astype(BF16)
        part = pl.ds(g * TILE, TILE)
        copies.append(pltpu.make_async_copy(fine_v.at[part], fine_out.at[part], sem.at[g]))
        copies[-1].start()
    for copy in copies:
        copy.wait()


def body(
    levels,
    fine_nodes,
    coarse_nodes,
    edge_latents,
    senders,
    receivers,
    live_blocks,
    send_list,
    parents,
    edge_weight,
    node_weights,
    out_weights,
    gains,
):
    arrays = (
        fine_nodes,
        coarse_nodes,
        edge_latents,
        senders.reshape(-1, LAT),
        receivers.reshape(-1, LAT),
        live_blocks,
        send_list.reshape(-1, SLOT),
        parents.reshape(-1, LAT),
        edge_weight,
        node_weights,
        out_weights,
        gains,
    )
    nodes, blocks, edges = fine_nodes.shape[0], coarse_nodes.shape[0], edge_latents.shape[0]
    groups, slots = nodes // TILE, send_list.shape[0] // SLOT
    inner = blocks - 2 * BORDER
    hbm = pl.BlockSpec(memory_space=pltpu.HBM)
    vmem = pl.BlockSpec(memory_space=pltpu.VMEM)
    held = [pltpu.VMEM(a.shape, a.dtype) for a in arrays]
    held[5] = pltpu.SMEM((1,), I32)
    edge_blocks = edges // group_edges
    state = pl.pallas_call(
        functools.partial(kernel, levels),
        out_shape=(
            pltpu.VMEM((nodes, LAT), BF16),
            pltpu.VMEM((nodes, LAT), F32),
            pltpu.VMEM((nodes, TILE), BF16),
            pltpu.VMEM((EDGE_ROWS, LAT), BF16),
            pltpu.VMEM((EDGE_ROWS, LAT), BF16),
            pltpu.VMEM((inner, LAT), BF16),
            pltpu.VMEM((2, 2 * LAT, LAT), BF16),
            pltpu.VMEM((2, 2 * LAT, LAT), BF16),
            pltpu.VMEM(gains.shape, F32),
        ),
        in_specs=[hbm] * 12,
        out_specs=(vmem,) * 9,
        scratch_shapes=held
        + [
            pltpu.VMEM((LAT, nodes + slots * SLOT), BF16),
            pltpu.VMEM((2 * LAT, nodes), F32),
            pltpu.VMEM((HALF, lane_tiles * LAT), I32),
            pltpu.VMEM((HALF, nodes), I32),
            pltpu.VMEM((edge_blocks, HALF, group_edges), I32),
            pltpu.VMEM((edge_blocks, LAT, group_edges), BF16),
            pltpu.VMEM((slots, LAT, SLOT), BF16),
            pltpu.VMEM((slots, LAT, SLOT), BF16),
            pltpu.VMEM((2 * TILE, LAT), BF16),
            pltpu.VMEM((nodes, TILE), BF16),
            pltpu.VMEM((2 * TILE, nodes), BF16),
            pltpu.VMEM((nodes, LAT), F32),
            pltpu.VMEM((2, 2 * BORDER, LAT), BF16),
            pltpu.VMEM((2, 2 * BORDER, LAT), BF16),
            pltpu.VMEM((groups * LAT, TILE), F32),
            pltpu.VMEM((2 * LAT, LAT), BF16),
            pltpu.VMEM((LAT, 2 * LAT), BF16),
            pltpu.VMEM((LAT, LAT), F32),
            pltpu.VMEM((LAT, LAT), F32),
            pltpu.SemaphoreType.DMA((12,)),
            pltpu.SemaphoreType.DMA((7,)),
            pltpu.SemaphoreType.DMA((7,)),
        ],
        compiler_params=pltpu.CompilerParams(
            collective_id=0, has_side_effects=True, vmem_limit_bytes=64_600_000
        ),
        name="graph_step",
    )(*arrays)
    return pl.pallas_call(
        finish,
        out_shape=(
            jax.ShapeDtypeStruct(fine_nodes.shape, BF16),
            jax.ShapeDtypeStruct(coarse_nodes.shape, BF16),
        ),
        in_specs=[vmem] * 9,
        out_specs=(hbm, hbm),
        scratch_shapes=[
            pltpu.VMEM(fine_nodes.shape, BF16),
            pltpu.VMEM(coarse_nodes.shape, BF16),
            pltpu.SemaphoreType.DMA((groups + 1,)),
        ],
        compiler_params=pltpu.CompilerParams(vmem_limit_bytes=16 * 1024 * 1024),
        name="graph_finish",
    )(*state)


def solution(mesh):
    both = ("region", "level")
    in_specs = (
        P(both, None),
        P(both, None),
        P(both, None),
        P(both),
        P(both),
        P(both),
        P(both),
        P(both),
        P(),
        P(),
        P(),
        P(),
    )
    return jax.shard_map(
        functools.partial(body, mesh.shape["level"]),
        mesh=mesh,
        in_specs=in_specs,
        out_specs=(P(both, None), P(both, None)),
        check_vma=False,
    )
```

```python
import functools

import jax
import jax.numpy as jnp
from jax import lax
from jax.experimental import pallas as pl
from jax.experimental.pallas import tpu as pltpu
from jax.sharding import PartitionSpec as P

MESH = pl.DeviceIdType.MESH
F32 = jnp.float32
BF16 = jnp.bfloat16
I32 = jnp.int32
LAT = 128
HALF = LAT // 2
BORDER = 64
EDGE_ROWS = 4 * BORDER
SLOT = 128
norm_eps = 1e-05
group_edges = 1024
sub = group_edges // LAT
TILE = 256
ahead = 2
lane_tiles = 4
top = 16380.0


def dot(a, b, ca=1, cb=0):
    return lax.dot_general(a, b, (((ca,), (cb,)), ((), ())), preferred_element_type=F32)


def half_silu(h):
    return (h * jnp.tanh(h) + h).astype(BF16)


def scale_rows(c):
    return c * lax.rsqrt(jnp.mean(c * c, axis=1, keepdims=True) + norm_eps)


def hot_columns(ids, rows):
    low, high = (ids & (TILE - 1)).astype(F32), ids >> 8
    shape = (TILE, ids.shape[1])
    place = lax.broadcasted_iota(I32, shape, 0).astype(BF16)
    parts = []
    for g in range(rows // TILE):
        mine = jnp.where(high == g, low, -1.0).astype(BF16)
        parts.append(
            jnp.where(place == jnp.broadcast_to(mine, shape), jnp.ones((), BF16), jnp.zeros((), BF16))
        )
    return jnp.concatenate(parts, axis=0)


def split(x, axis):
    high = x.astype(BF16)
    return jnp.concatenate([high, (x - high.astype(F32)).astype(BF16)], axis=axis)


def centered(w):
    wide = w.astype(F32)
    return split(wide - jnp.mean(wide, axis=1, keepdims=True), 0)


def twice(x, axis=1):
    return jnp.concatenate([x, x], axis=axis)


def kernel(
    levels,
    fine_h,
    coarse_h,
    latents_h,
    senders_h,
    receivers_h,
    live_h,
    send_list_h,
    parents_h,
    edge_w_h,
    node_w_h,
    out_w_h,
    gains_h,
    mid,
    down_pre,
    par_edge,
    base_edge,
    total_edge,
    new_inner,
    late_w,
    late_out,
    late_gain,
    fine,
    coarse,
    latents,
    senders,
    receivers,
    live,
    send_list,
    parents,
    edge_w,
    node_w,
    out_w,
    gains,
    table,
    full,
    sender_q,
    receiver_q,
    packed,
    acts,
    outgoing,
    arrived,
    cext,
    par_inner,
    par_near,
    par_cols,
    up_pre,
    sums_out,
    sums_in,
    acc,
    first_t,
    second_t,
    gain_t,
    scale_t,
    load_sem,
    send_sem,
    recv_sem,
):
    r, l = lax.axis_index("region"), lax.axis_index("level")
    nodes, blocks = fine.shape[0], coarse.shape[0]
    inner = blocks - 2 * BORDER
    ext = blocks + 2 * BORDER
    groups = nodes // TILE
    slots = arrived.shape[0]
    edge_blocks = latents.shape[0] // group_edges
    has_lower, has_upper = l > 0, l < levels - 1
    lower, upper, peer = (r, l - 1), (r, l + 1), (1 - r, l)

    barrier = pltpu.get_barrier_semaphore()
    pl.semaphore_signal(barrier, inc=1, device_id=peer, device_id_type=MESH)

    @pl.when(has_lower)
    def _():
        pl.semaphore_signal(barrier, inc=1, device_id=lower, device_id_type=MESH)

    @pl.when(has_upper)
    def _():
        pl.semaphore_signal(barrier, inc=1, device_id=upper, device_id_type=MESH)

    pairs = [
        (edge_w_h, edge_w),
        (fine_h, fine),
        (send_list_h, send_list),
        (coarse_h, coarse),
        (receivers_h, receivers),
        (senders_h, senders),
        (parents_h, parents),
        (latents_h, latents),
        (out_w_h, out_w),
        (gains_h, gains),
        (node_w_h, node_w),
        (live_h, live),
    ]
    loads = [pltpu.make_async_copy(s, d, load_sem.at[k]) for k, (s, d) in enumerate(pairs)]
    for load in loads:
        load.start()

    def remote(kind, src, dst, device):
        return pltpu.make_async_remote_copy(
            src_ref=src,
            dst_ref=dst,
            send_sem=send_sem.at[kind],
            recv_sem=recv_sem.at[kind],
            device_id=device,
            device_id_type=MESH,
        )

    halo_down = remote(0, outgoing.at[0], arrived.at[1], lower)
    halo_up = remote(1, outgoing.at[1], arrived.at[0], upper)
    halo_peer = remote(2, outgoing.at[3 - r], arrived.at[2 + r], peer)
    coarse_down = remote(3, coarse.at[pl.ds(0, BORDER)], cext.at[pl.ds(3 * BORDER, BORDER)], lower)
    coarse_up = remote(4, coarse.at[pl.ds(blocks - BORDER, BORDER)], cext.at[pl.ds(0, BORDER)], upper)
    sums_down = remote(5, sums_out.at[0], sums_in.at[1], lower)
    sums_up = remote(6, sums_out.at[1], sums_in.at[0], upper)

    loads[0].wait()
    w_both = jnp.concatenate(
        [
            (edge_w[LAT : 2 * LAT, :].astype(F32) * 0.5).T.astype(BF16),
            (edge_w[2 * LAT :, :].astype(F32) * 0.5).T.astype(BF16),
        ],
        axis=0,
    )
    loads[1].wait()
    for g in range(groups):
        both = dot(w_both, fine[g * TILE : (g + 1) * TILE, :], 1, 1)
        full[:, g * TILE : (g + 1) * TILE] = both
        table[:, g * TILE : (g + 1) * TILE] = both[:LAT].astype(BF16)

    loads[2].wait()
    sends = jnp.concatenate([send_list[j : j + 1, :] for j in range(slots)], axis=1)
    picked = dot(table[:, :nodes], hot_columns(sends, nodes)).astype(BF16)
    for j in range(slots):
        outgoing[j] = picked[:, j * SLOT : (j + 1) * SLOT]
    loads[3].wait()

    pl.semaphore_wait(barrier, 1 + has_lower.astype(I32) + has_upper.astype(I32))

    @pl.when(has_lower)
    def _():
        halo_down.start()

    @pl.when(has_upper)
    def _():
        halo_up.start()

    halo_peer.start()

    @pl.when(has_lower)
    def _():
        coarse_down.start()

    @pl.when(has_upper)
    def _():
        coarse_up.start()

    arrived[2 + r] = outgoing[2 + r]
    cext[BORDER : 2 * BORDER, :] = coarse[:BORDER, :]
    cext[2 * BORDER : 3 * BORDER, :] = coarse[blocks - BORDER :, :]
    cext[EDGE_ROWS : EDGE_ROWS + inner, :] = coarse[BORDER : blocks - BORDER, :]
    cext[EDGE_ROWS + inner :, :] = jnp.zeros((cext.shape[0] - EDGE_ROWS - inner, LAT), BF16)

    @pl.when(jnp.logical_not(has_lower))
    def _():
        arrived[0] = jnp.zeros((LAT, SLOT), BF16)
        cext[:BORDER, :] = jnp.zeros((BORDER, LAT), BF16)
        sums_in[0] = jnp.zeros((2 * BORDER, LAT), BF16)

    @pl.when(jnp.logical_not(has_upper))
    def _():
        arrived[1] = jnp.zeros((LAT, SLOT), BF16)
        cext[3 * BORDER : 4 * BORDER, :] = jnp.zeros((BORDER, LAT), BF16)
        sums_in[1] = jnp.zeros((2 * BORDER, LAT), BF16)

    most = jnp.max(jnp.abs(full[...]), axis=1, keepdims=True)
    most = jnp.maximum(jnp.maximum(most[:LAT], most[LAT:]), 1e-30)
    step = most * (1.0 / top)
    scale_t[...] = jnp.broadcast_to(step * (1.0 / 65536.0), (LAT, LAT))
    inverse = top / most

    def pack(start, count, target):
        for t in range(count):
            cols = slice(t * LAT, (t + 1) * LAT)
            q = full[start : start + LAT, cols] * inverse
            low = jnp.round(q[HALF:])
            high = jnp.round(q[:HALF] - low * (1.0 / 65536.0))
            target[:, cols] = high.astype(I32) * 65536 + low.astype(I32)

    pack(0, lane_tiles, sender_q)
    pack(LAT, nodes // LAT, receiver_q)

    def gather(b):
        for j in range(sub):

            def look_up(ids, target, x, count):
                low = jnp.broadcast_to(ids & (LAT - 1), (HALF, LAT))
                high = jnp.broadcast_to(ids >> 7, (HALF, LAT))
                for t in range(count):
                    found = jnp.take_along_axis(target[:, t * LAT : (t + 1) * LAT], low, axis=1)
                    x = found if x is None else jnp.where(high == t, found, x)
                return x

            s, t = senders[pl.ds(b * sub + j, 1), :], receivers[pl.ds(b * sub + j, 1), :]
            total = look_up(t, receiver_q, None, nodes // LAT)
            total = total + look_up(s, sender_q, jnp.zeros((HALF, LAT), I32), lane_tiles)
            packed[b, :, j * LAT : (j + 1) * LAT] = total

    loads[4].wait()
    loads[5].wait()

    def gather_step(b, carry):
        gather(b)
        return carry

    lax.fori_loop(0, ahead, gather_step, 0)

    loads[6].wait()
    offset = BORDER - l * blocks
    for j in range(nodes // LAT):
        p = parents[j : j + 1, :] + offset
        p = jnp.where(
            p < 2 * BORDER, p, jnp.where(p < 2 * BORDER + inner, p + 2 * BORDER, p - inner)
        )
        par_cols[:, j * LAT : (j + 1) * LAT] = hot_columns(p, par_cols.shape[0])
        column = jnp.broadcast_to(p.astype(F32), (LAT, LAT)).T
        ids = lax.broadcasted_iota(I32, (LAT, LAT), 1).astype(F32)
        rows = slice(j * LAT, (j + 1) * LAT)
        for k in range(2):
            cols = slice(k * LAT, (k + 1) * LAT)
            par_edge[rows, cols] = jnp.where(ids + float(k * LAT) == column, 1.0, 0.0).astype(BF16)
            par_inner[rows, cols] = jnp.where(
                ids + float(EDGE_ROWS + k * LAT) == column, 1.0, 0.0
            ).astype(BF16)
        near = jnp.where(ids < float(BORDER), ids, ids + float(2 * BORDER))
        par_near[rows, :] = jnp.where(near == column, 1.0, 0.0).astype(BF16)

    for k in range(7, 12):
        loads[k].wait()
    first_t[:LAT, :] = (edge_w[:LAT, :].astype(F32) * 0.5).T.astype(BF16)
    eye = lax.broadcasted_iota(I32, (LAT, LAT), 0) == lax.broadcasted_iota(I32, (LAT, LAT), 1)
    first_t[LAT:, :] = jnp.where(eye, 1.0, 0.0).astype(BF16)
    wide = out_w[0].astype(F32).T
    second_t[...] = split(wide - jnp.mean(wide, axis=0, keepdims=True), 1)
    gain_t[...] = jnp.broadcast_to(gains[0:1, :], (LAT, LAT)).T
    acc[...] = jnp.zeros_like(acc)
    late_w[...] = node_w[2:4]
    late_out[0] = centered(out_w[3])
    late_out[1] = centered(out_w[4])
    late_gain[...] = gains[...]

    none = jnp.zeros((BORDER, LAT), BF16)
    own_edge = jnp.concatenate([none, coarse[:BORDER, :], coarse[blocks - BORDER :, :], none], axis=0)
    edge_table = split(dot(own_edge, node_w[1, LAT:, :]), 1)
    inner_table = split(dot(cext[EDGE_ROWS:, :], node_w[1, LAT:, :]), 1)
    for g in range(groups):
        rows = slice(g * TILE, (g + 1) * TILE)
        found = dot(par_edge[rows, :], edge_table) + dot(par_inner[rows, :], inner_table)
        up_pre[rows, :] = found[:, :LAT] + found[:, LAT:]

    halo_peer.wait()

    @pl.when(has_lower)
    def _():
        halo_down.wait_send()
        halo_up.wait_recv()
        coarse_down.wait_send()
        coarse_up.wait_recv()

    @pl.when(has_upper)
    def _():
        halo_up.wait_send()
        halo_down.wait_recv()
        coarse_up.wait_send()
        coarse_down.wait_recv()

    for j in range(slots):
        table[:, nodes + j * SLOT : nodes + (j + 1) * SLOT] = arrived[j]

    gain_all = jnp.concatenate([gain_t[...]] * sub, axis=1)
    scale_all = jnp.concatenate([scale_t[...]] * sub, axis=1)
    skip = lane_tiles * LAT
    listed = table.shape[1]

    def row(ref, b):
        return jnp.concatenate([ref[pl.ds(b * sub + j, 1), :] for j in range(sub)], axis=1)

    def block(b):
        return latents[pl.ds(pl.multiple_of(b * group_edges, group_edges), group_edges), :]

    def hidden_layer(b):
        h = dot(first_t[:LAT, :], block(b), 1, 1)
        h = h + dot(table[:, skip:], hot_columns(row(senders, b) - skip, listed - skip))
        own = packed[b]
        own = jnp.concatenate([own.astype(F32), (own << 16).astype(F32)], axis=0)
        acts[b] = half_silu(h + own * scale_all)

    def add_edges(b):
        lat = dot(first_t[LAT:, :], block(b), 1, 1)
        c = dot(second_t[...], twice(acts[b], 0))
        spread = lax.rsqrt(jnp.mean(c * c, axis=0, keepdims=True) + norm_eps)
        updated = (lat + c * spread * gain_all).astype(BF16)
        ids = row(receivers, b)
        position = b * group_edges + lax.broadcasted_iota(I32, (1, group_edges), 1)
        target = jnp.where(position < live[0] * 128, ids >> 8, groups)
        masked = jnp.concatenate(
            [
                updated
                * jnp.broadcast_to(jnp.where(target == g, 1.0, 0.0).astype(BF16), updated.shape)
                for g in range(groups)
            ],
            axis=0,
        )
        acc[...] += dot(masked, hot_columns(ids & (TILE - 1), TILE), 1, 1)

    hidden_layer(0)

    def full_step(b, carry):
        add_edges(b)
        hidden_layer(b + 1)
        gather(b + ahead)
        return carry

    def last_step(b, carry):
        add_edges(b)
        hidden_layer(b + 1)
        return carry

    lax.fori_loop(0, edge_blocks - ahead, full_step, 0)
    lax.fori_loop(edge_blocks - ahead, edge_blocks - 1, last_step, 0)
    add_edges(edge_blocks - 1)

    fine_out_w, up_out_w = centered(out_w[1]), centered(out_w[2])
    near = jnp.concatenate([cext[:BORDER, :], cext[3 * BORDER : EDGE_ROWS, :]], axis=0)
    near_table = dot(near, node_w[1, LAT:, :]).astype(BF16)
    up_w = jnp.concatenate([node_w[1, :LAT, :], near_table], axis=0)
    parts = [slice(g * TILE, (g + 1) * TILE) for g in range(groups)]
    aggs = [acc[g * LAT : (g + 1) * LAT, :].T.astype(BF16) for g in range(groups)]
    hs = [
        dot(jnp.concatenate([fine[p, :], agg], axis=1), node_w[0]) for p, agg in zip(parts, aggs)
    ]
    cs = [dot(twice(half_silu(0.5 * h)), fine_out_w) for h in hs]
    news = [
        (fine[p, :].astype(F32) + scale_rows(c) * gains[1:2, :]).astype(BF16)
        for p, c in zip(parts, cs)
    ]
    for p, new in zip(parts, news):
        mid[p, :] = new
    hs = [
        dot(jnp.concatenate([new, par_near[p, :]], axis=1), up_w) + up_pre[p, :]
        for p, new in zip(parts, news)
    ]
    cs = [dot(twice(half_silu(0.5 * h)), up_out_w) for h in hs]
    ups = jnp.concatenate([split(scale_rows(c) * gains[2:3, :], 1) for c in cs], axis=0)
    sums = dot(par_cols[...], ups)
    sums = sums[:, :LAT] + sums[:, LAT:]
    sums_out[0] = sums[: 2 * BORDER].astype(BF16)
    sums_out[1] = sums[2 * BORDER : EDGE_ROWS].astype(BF16)

    @pl.when(has_lower)
    def _():
        sums_down.start()

    @pl.when(has_upper)
    def _():
        sums_up.start()

    base = cext[EDGE_ROWS:, :]
    h = dot(jnp.concatenate([base, sums[EDGE_ROWS:].astype(BF16)], axis=1), node_w[2])
    new = scale_rows(dot(twice(half_silu(0.5 * h)), late_out[0])) * gains[3:4, :]
    new = (base.astype(F32) + new).astype(BF16)
    new_inner[...] = new[:inner]
    inner_table = split(dot(new, node_w[3, LAT:, :]), 1)
    for g in range(groups):
        rows = slice(g * TILE, (g + 1) * TILE)
        found = dot(par_inner[rows, :], inner_table)
        down_pre[rows, :] = dot(mid[rows, :], node_w[3, :LAT, :]) + (found[:, :LAT] + found[:, LAT:])
    base_edge[...] = cext[:EDGE_ROWS, :]

    @pl.when(has_lower)
    def _():
        sums_down.wait_send()
        sums_up.wait_recv()

    @pl.when(has_upper)
    def _():
        sums_up.wait_send()
        sums_down.wait_recv()

    total_edge[: 2 * BORDER, :] = (sums[: 2 * BORDER] + sums_in[0].astype(F32)).astype(BF16)
    total_edge[2 * BORDER :, :] = (sums[2 * BORDER : EDGE_ROWS] + sums_in[1].astype(F32)).astype(BF16)


def finish(
    mid,
    down_pre,
    par_edge,
    base_edge,
    total_edge,
    new_inner,
    late_w,
    late_out,
    late_gain,
    fine_out,
    coarse_out,
    fine_v,
    coarse_v,
    sem,
):
    nodes, blocks = fine_v.shape[0], coarse_v.shape[0]
    base = base_edge[...]
    h = dot(jnp.concatenate([base, total_edge[...]], axis=1), late_w[0])
    new = scale_rows(dot(twice(half_silu(0.5 * h)), late_out[0])) * late_gain[3:4, :]
    new = (base.astype(F32) + new).astype(BF16)
    coarse_v[:BORDER, :] = new[BORDER : 2 * BORDER]
    coarse_v[blocks - BORDER :, :] = new[2 * BORDER : 3 * BORDER]
    coarse_v[BORDER : blocks - BORDER, :] = new_inner[...]
    copies = [pltpu.make_async_copy(coarse_v, coarse_out, sem.at[nodes // TILE])]
    copies[0].start()
    edge_table = split(dot(new, late_w[1, LAT:, :]), 1)
    parts = [slice(g * TILE, (g + 1) * TILE) for g in range(nodes // TILE)]
    found = [dot(par_edge[p, :], edge_table) for p in parts]
    hs = [down_pre[p, :] + (f[:, :LAT] + f[:, LAT:]) for p, f in zip(parts, found)]
    cs = [dot(twice(half_silu(0.5 * h)), late_out[1]) for h in hs]
    for g, c in enumerate(cs):
        p = parts[g]
        new = scale_rows(c) * late_gain[4:5, :]
        fine_v[p, :] = (mid[p, :].astype(F32) + new).astype(BF16)
        part = pl.ds(g * TILE, TILE)
        copies.append(pltpu.make_async_copy(fine_v.at[part], fine_out.at[part], sem.at[g]))
        copies[-1].start()
    for copy in copies:
        copy.wait()


def body(
    levels,
    fine_nodes,
    coarse_nodes,
    edge_latents,
    senders,
    receivers,
    live_blocks,
    send_list,
    parents,
    edge_weight,
    node_weights,
    out_weights,
    gains,
):
    arrays = (
        fine_nodes,
        coarse_nodes,
        edge_latents,
        senders.reshape(-1, LAT),
        receivers.reshape(-1, LAT),
        live_blocks,
        send_list.reshape(-1, SLOT),
        parents.reshape(-1, LAT),
        edge_weight,
        node_weights,
        out_weights,
        gains,
    )
    nodes, blocks, edges = fine_nodes.shape[0], coarse_nodes.shape[0], edge_latents.shape[0]
    groups, slots = nodes // TILE, send_list.shape[0] // SLOT
    inner = blocks - 2 * BORDER
    hbm = pl.BlockSpec(memory_space=pltpu.HBM)
    vmem = pl.BlockSpec(memory_space=pltpu.VMEM)
    held = [pltpu.VMEM(a.shape, a.dtype) for a in arrays]
    held[5] = pltpu.SMEM((1,), I32)
    edge_blocks = edges // group_edges
    state = pl.pallas_call(
        functools.partial(kernel, levels),
        out_shape=(
            pltpu.VMEM((nodes, LAT), BF16),
            pltpu.VMEM((nodes, LAT), F32),
            pltpu.VMEM((nodes, TILE), BF16),
            pltpu.VMEM((EDGE_ROWS, LAT), BF16),
            pltpu.VMEM((EDGE_ROWS, LAT), BF16),
            pltpu.VMEM((inner, LAT), BF16),
            pltpu.VMEM((2, 2 * LAT, LAT), BF16),
            pltpu.VMEM((2, 2 * LAT, LAT), BF16),
            pltpu.VMEM(gains.shape, F32),
        ),
        in_specs=[hbm] * 12,
        out_specs=(vmem,) * 9,
        scratch_shapes=held
        + [
            pltpu.VMEM((LAT, nodes + slots * SLOT), BF16),
            pltpu.VMEM((2 * LAT, nodes), F32),
            pltpu.VMEM((HALF, lane_tiles * LAT), I32),
            pltpu.VMEM((HALF, nodes), I32),
            pltpu.VMEM((edge_blocks, HALF, group_edges), I32),
            pltpu.VMEM((edge_blocks, LAT, group_edges), BF16),
            pltpu.VMEM((slots, LAT, SLOT), BF16),
            pltpu.VMEM((slots, LAT, SLOT), BF16),
            pltpu.VMEM((2 * TILE, LAT), BF16),
            pltpu.VMEM((nodes, TILE), BF16),
            pltpu.VMEM((nodes, 2 * BORDER), BF16),
            pltpu.VMEM((2 * TILE, nodes), BF16),
            pltpu.VMEM((nodes, LAT), F32),
            pltpu.VMEM((2, 2 * BORDER, LAT), BF16),
            pltpu.VMEM((2, 2 * BORDER, LAT), BF16),
            pltpu.VMEM((groups * LAT, TILE), F32),
            pltpu.VMEM((2 * LAT, LAT), BF16),
            pltpu.VMEM((LAT, 2 * LAT), BF16),
            pltpu.VMEM((LAT, LAT), F32),
            pltpu.VMEM((LAT, LAT), F32),
            pltpu.SemaphoreType.DMA((12,)),
            pltpu.SemaphoreType.DMA((7,)),
            pltpu.SemaphoreType.DMA((7,)),
        ],
        compiler_params=pltpu.CompilerParams(
            collective_id=0, has_side_effects=True, vmem_limit_bytes=64_600_000
        ),
        name="graph_step",
    )(*arrays)
    return pl.pallas_call(
        finish,
        out_shape=(
            jax.ShapeDtypeStruct(fine_nodes.shape, BF16),
            jax.ShapeDtypeStruct(coarse_nodes.shape, BF16),
        ),
        in_specs=[vmem] * 9,
        out_specs=(hbm, hbm),
        scratch_shapes=[
            pltpu.VMEM(fine_nodes.shape, BF16),
            pltpu.VMEM(coarse_nodes.shape, BF16),
            pltpu.SemaphoreType.DMA((groups + 1,)),
        ],
        compiler_params=pltpu.CompilerParams(vmem_limit_bytes=16 * 1024 * 1024),
        name="graph_finish",
    )(*state)


def solution(mesh):
    both = ("region", "level")
    in_specs = (
        P(both, None),
        P(both, None),
        P(both, None),
        P(both),
        P(both),
        P(both),
        P(both),
        P(both),
        P(),
        P(),
        P(),
        P(),
    )
    return jax.shard_map(
        functools.partial(body, mesh.shape["level"]),
        mesh=mesh,
        in_specs=in_specs,
        out_specs=(P(both, None), P(both, None)),
        check_vma=False,
    )
```

```python
import functools

import jax
import jax.numpy as jnp
from jax import lax
from jax.experimental import pallas as pl
from jax.experimental.pallas import tpu as pltpu
from jax.sharding import PartitionSpec as P

MESH = pl.DeviceIdType.MESH
F32 = jnp.float32
BF16 = jnp.bfloat16
I32 = jnp.int32
LAT = 128
HALF = LAT // 2
BORDER = 64
EDGE_ROWS = 4 * BORDER
SLOT = 128
norm_eps = 1e-05
group_edges = 1024
sub = group_edges // LAT
TILE = 256
ahead = 2
lane_tiles = 4
top = 16380.0


def dot(a, b, ca=1, cb=0):
    return lax.dot_general(a, b, (((ca,), (cb,)), ((), ())), preferred_element_type=F32)


def half_silu(h):
    return (h * jnp.tanh(h) + h).astype(BF16)


def scale_rows(c):
    return c * lax.rsqrt(jnp.mean(c * c, axis=1, keepdims=True) + norm_eps)


def hot_columns(ids, rows):
    low, high = (ids & (TILE - 1)).astype(F32), ids >> 8
    shape = (TILE, ids.shape[1])
    place = lax.broadcasted_iota(I32, shape, 0).astype(BF16)
    parts = []
    for g in range(rows // TILE):
        mine = jnp.where(high == g, low, -1.0).astype(BF16)
        parts.append(
            jnp.where(place == jnp.broadcast_to(mine, shape), jnp.ones((), BF16), jnp.zeros((), BF16))
        )
    return jnp.concatenate(parts, axis=0)


def split(x, axis):
    high = x.astype(BF16)
    return jnp.concatenate([high, (x - high.astype(F32)).astype(BF16)], axis=axis)


def centered(w):
    wide = w.astype(F32)
    return split(wide - jnp.mean(wide, axis=1, keepdims=True), 0)


def twice(x, axis=1):
    return jnp.concatenate([x, x], axis=axis)


def orders(w):
    return w, jnp.concatenate([w[LAT:], w[:LAT]], axis=0)


def ordered(a, b, part):
    return jnp.concatenate([a, b] if part % 2 == 0 else [b, a], axis=1)


def swapped(w):
    return w, jnp.concatenate([w[:, LAT:], w[:, :LAT]], axis=1)


def kernel(
    levels,
    fine_h,
    coarse_h,
    latents_h,
    senders_h,
    receivers_h,
    live_h,
    send_list_h,
    parents_h,
    edge_w_h,
    node_w_h,
    out_w_h,
    gains_h,
    mid,
    down_pre,
    par_edge,
    base_edge,
    total_edge,
    new_inner,
    late_w,
    late_out,
    late_gain,
    fine,
    coarse,
    latents,
    senders,
    receivers,
    live,
    send_list,
    parents,
    edge_w,
    node_w,
    out_w,
    gains,
    table,
    full,
    sender_q,
    receiver_q,
    packed,
    acts,
    outgoing,
    arrived,
    cext,
    par_inner,
    par_near,
    par_cols,
    up_pre,
    sums_out,
    sums_in,
    sums_v,
    acc,
    first_t,
    second_t,
    gain_t,
    scale_t,
    load_sem,
    send_sem,
    recv_sem,
):
    r, l = lax.axis_index("region"), lax.axis_index("level")
    nodes, blocks = fine.shape[0], coarse.shape[0]
    inner = blocks - 2 * BORDER
    ext = blocks + 2 * BORDER
    groups = nodes // TILE
    slots = arrived.shape[0]
    edge_blocks = latents.shape[0] // group_edges
    has_lower, has_upper = l > 0, l < levels - 1
    lower, upper, peer = (r, l - 1), (r, l + 1), (1 - r, l)

    barrier = pltpu.get_barrier_semaphore()
    pl.semaphore_signal(barrier, inc=1, device_id=peer, device_id_type=MESH)

    @pl.when(has_lower)
    def _():
        pl.semaphore_signal(barrier, inc=1, device_id=lower, device_id_type=MESH)

    @pl.when(has_upper)
    def _():
        pl.semaphore_signal(barrier, inc=1, device_id=upper, device_id_type=MESH)

    pairs = [
        (edge_w_h, edge_w),
        (fine_h, fine),
        (send_list_h, send_list),
        (coarse_h, coarse),
        (receivers_h, receivers),
        (senders_h, senders),
        (parents_h, parents),
        (latents_h, latents),
        (out_w_h, out_w),
        (gains_h, gains),
        (node_w_h, node_w),
        (live_h, live),
    ]
    loads = [pltpu.make_async_copy(s, d, load_sem.at[k]) for k, (s, d) in enumerate(pairs)]
    for load in loads:
        load.start()

    def remote(kind, src, dst, device):
        return pltpu.make_async_remote_copy(
            src_ref=src,
            dst_ref=dst,
            send_sem=send_sem.at[kind],
            recv_sem=recv_sem.at[kind],
            device_id=device,
            device_id_type=MESH,
        )

    halo_down = remote(0, outgoing.at[0], arrived.at[1], lower)
    halo_up = remote(1, outgoing.at[1], arrived.at[0], upper)
    halo_peer = remote(2, outgoing.at[3 - r], arrived.at[2 + r], peer)
    coarse_down = remote(3, coarse.at[pl.ds(0, BORDER)], cext.at[pl.ds(3 * BORDER, BORDER)], lower)
    coarse_up = remote(4, coarse.at[pl.ds(blocks - BORDER, BORDER)], cext.at[pl.ds(0, BORDER)], upper)
    sums_down = remote(5, sums_out.at[0], sums_in.at[1], lower)
    sums_up = remote(6, sums_out.at[1], sums_in.at[0], upper)

    loads[0].wait()
    w_both = jnp.concatenate(
        [
            (edge_w[LAT : 2 * LAT, :].astype(F32) * 0.5).T.astype(BF16),
            (edge_w[2 * LAT :, :].astype(F32) * 0.5).T.astype(BF16),
        ],
        axis=0,
    )
    loads[1].wait()
    for g in range(groups):
        both = dot(w_both, fine[g * TILE : (g + 1) * TILE, :], 1, 1)
        full[:, g * TILE : (g + 1) * TILE] = both
        table[:, g * TILE : (g + 1) * TILE] = both[:LAT].astype(BF16)

    loads[2].wait()
    sends = jnp.concatenate([send_list[j : j + 1, :] for j in range(slots)], axis=1)
    picked = dot(table[:, :nodes], hot_columns(sends, nodes)).astype(BF16)
    for j in range(slots):
        outgoing[j] = picked[:, j * SLOT : (j + 1) * SLOT]
    loads[3].wait()

    pl.semaphore_wait(barrier, 1 + has_lower.astype(I32) + has_upper.astype(I32))

    @pl.when(has_lower)
    def _():
        halo_down.start()

    @pl.when(has_upper)
    def _():
        halo_up.start()

    halo_peer.start()

    @pl.when(has_lower)
    def _():
        coarse_down.start()

    @pl.when(has_upper)
    def _():
        coarse_up.start()

    arrived[2 + r] = outgoing[2 + r]
    cext[BORDER : 2 * BORDER, :] = coarse[:BORDER, :]
    cext[2 * BORDER : 3 * BORDER, :] = coarse[blocks - BORDER :, :]
    cext[EDGE_ROWS : EDGE_ROWS + inner, :] = coarse[BORDER : blocks - BORDER, :]
    cext[EDGE_ROWS + inner :, :] = jnp.zeros((cext.shape[0] - EDGE_ROWS - inner, LAT), BF16)

    @pl.when(jnp.logical_not(has_lower))
    def _():
        arrived[0] = jnp.zeros((LAT, SLOT), BF16)
        cext[:BORDER, :] = jnp.zeros((BORDER, LAT), BF16)
        sums_in[0] = jnp.zeros((2 * BORDER, LAT), BF16)

    @pl.when(jnp.logical_not(has_upper))
    def _():
        arrived[1] = jnp.zeros((LAT, SLOT), BF16)
        cext[3 * BORDER : 4 * BORDER, :] = jnp.zeros((BORDER, LAT), BF16)
        sums_in[1] = jnp.zeros((2 * BORDER, LAT), BF16)

    most = jnp.max(jnp.abs(full[...]), axis=1, keepdims=True)
    most = jnp.maximum(jnp.maximum(most[:LAT], most[LAT:]), 1e-30)
    step = most * (1.0 / top)
    scale_t[...] = jnp.broadcast_to(step * (1.0 / 65536.0), (LAT, LAT))
    inverse = top / most

    def pack(start, count, target):
        for t in range(count):
            cols = slice(t * LAT, (t + 1) * LAT)
            q = full[start : start + LAT, cols] * inverse
            low = jnp.round(q[HALF:])
            high = jnp.round(q[:HALF] - low * (1.0 / 65536.0))
            target[:, cols] = high.astype(I32) * 65536 + low.astype(I32)

    pack(0, lane_tiles, sender_q)
    pack(LAT, nodes // LAT, receiver_q)

    def gather(b):
        for j in range(sub):

            def look_up(ids, target, x, count):
                low = jnp.broadcast_to(ids & (LAT - 1), (HALF, LAT))
                high = jnp.broadcast_to(ids >> 7, (HALF, LAT))
                for t in range(count):
                    found = jnp.take_along_axis(target[:, t * LAT : (t + 1) * LAT], low, axis=1)
                    x = found if x is None else jnp.where(high == t, found, x)
                return x

            s, t = senders[pl.ds(b * sub + j, 1), :], receivers[pl.ds(b * sub + j, 1), :]
            total = look_up(t, receiver_q, None, nodes // LAT)
            total = total + look_up(s, sender_q, jnp.zeros((HALF, LAT), I32), lane_tiles)
            packed[b, :, j * LAT : (j + 1) * LAT] = total

    loads[4].wait()
    loads[5].wait()

    def gather_step(b, carry):
        gather(b)
        return carry

    lax.fori_loop(0, ahead, gather_step, 0)

    loads[6].wait()
    offset = BORDER - l * blocks
    for j in range(nodes // LAT):
        p = parents[j : j + 1, :] + offset
        p = jnp.where(
            p < 2 * BORDER, p, jnp.where(p < 2 * BORDER + inner, p + 2 * BORDER, p - inner)
        )
        par_cols[:, j * LAT : (j + 1) * LAT] = hot_columns(p, par_cols.shape[0])
        column = jnp.broadcast_to(p.astype(F32), (LAT, LAT)).T
        ids = lax.broadcasted_iota(I32, (LAT, LAT), 1).astype(F32)
        rows = slice(j * LAT, (j + 1) * LAT)
        for k in range(2):
            cols = slice(k * LAT, (k + 1) * LAT)
            par_edge[rows, cols] = jnp.where(ids + float(k * LAT) == column, 1.0, 0.0).astype(BF16)
            par_inner[rows, cols] = jnp.where(
                ids + float(EDGE_ROWS + k * LAT) == column, 1.0, 0.0
            ).astype(BF16)
        near = jnp.where(ids < float(BORDER), ids, ids + float(2 * BORDER))
        par_near[rows, :] = jnp.where(near == column, 1.0, 0.0).astype(BF16)

    for k in range(7, 12):
        loads[k].wait()
    first_t[:LAT, :] = (edge_w[:LAT, :].astype(F32) * 0.5).T.astype(BF16)
    eye = lax.broadcasted_iota(I32, (LAT, LAT), 0) == lax.broadcasted_iota(I32, (LAT, LAT), 1)
    first_t[LAT:, :] = jnp.where(eye, 1.0, 0.0).astype(BF16)
    wide = out_w[0].astype(F32).T
    second_t[...] = split(wide - jnp.mean(wide, axis=0, keepdims=True), 1)
    gain_t[...] = jnp.broadcast_to(gains[0:1, :], (LAT, LAT)).T
    acc[...] = jnp.zeros_like(acc)
    late_w[...] = node_w[2:4]
    late_out[0] = centered(out_w[3])
    late_out[1] = centered(out_w[4])
    late_gain[...] = gains[...]

    none = jnp.zeros((BORDER, LAT), BF16)
    own_edge = jnp.concatenate([none, coarse[:BORDER, :], coarse[blocks - BORDER :, :], none], axis=0)
    edge_table = split(dot(own_edge, node_w[1, LAT:, :]), 1)
    inner_table = split(dot(cext[EDGE_ROWS:, :], node_w[1, LAT:, :]), 1)
    for g in range(groups):
        rows = slice(g * TILE, (g + 1) * TILE)
        found = dot(par_edge[rows, :], edge_table) + dot(par_inner[rows, :], inner_table)
        up_pre[rows, :] = found[:, :LAT] + found[:, LAT:]

    halo_peer.wait()

    @pl.when(has_lower)
    def _():
        halo_down.wait_send()
        halo_up.wait_recv()
        coarse_down.wait_send()
        coarse_up.wait_recv()

    @pl.when(has_upper)
    def _():
        halo_up.wait_send()
        halo_down.wait_recv()
        coarse_up.wait_send()
        coarse_down.wait_recv()

    for j in range(slots):
        table[:, nodes + j * SLOT : nodes + (j + 1) * SLOT] = arrived[j]

    gain_all = jnp.concatenate([gain_t[...]] * sub, axis=1)
    scale_all = jnp.concatenate([scale_t[...]] * sub, axis=1)
    skip = lane_tiles * LAT
    listed = table.shape[1]

    def row(ref, b):
        return jnp.concatenate([ref[pl.ds(b * sub + j, 1), :] for j in range(sub)], axis=1)

    def block(b):
        return latents[pl.ds(pl.multiple_of(b * group_edges, group_edges), group_edges), :]

    def hidden_layer(b):
        h = dot(first_t[:LAT, :], block(b), 1, 1)
        h = h + dot(table[:, skip:], hot_columns(row(senders, b) - skip, listed - skip))
        own = packed[b]
        own = jnp.concatenate([own.astype(F32), (own << 16).astype(F32)], axis=0)
        acts[b] = half_silu(h + own * scale_all)

    def add_edges(b, cut=group_edges):
        lat = dot(first_t[LAT:, :], block(b), 1, 1)
        c = dot(second_t[...], twice(acts[b], 0))
        spread = lax.rsqrt(jnp.mean(c * c, axis=0, keepdims=True) + norm_eps)
        updated = (lat + c * spread * gain_all).astype(BF16)
        ids = row(receivers, b)
        position = b * group_edges + lax.broadcasted_iota(I32, (1, group_edges), 1)
        target = jnp.where(position < live[0] * 128, ids >> 8, groups)
        masks = [jnp.where(target == g, 1.0, 0.0).astype(BF16) for g in range(groups)]
        hot = hot_columns(ids & (TILE - 1), TILE)

        def summed(cols):
            part = updated[:, cols]
            masked = [part * jnp.broadcast_to(mask[:, cols], part.shape) for mask in masks]
            return dot(jnp.concatenate(masked, axis=0), hot[:, cols], 1, 1)

        total = summed(slice(0, cut))
        if cut < group_edges:
            total = total + summed(slice(cut, group_edges))
        acc[...] += total

    hidden_layer(0)

    def full_step(b, carry):
        add_edges(b)
        hidden_layer(b + 1)
        gather(b + ahead)
        return carry

    def last_step(b, carry):
        add_edges(b)
        hidden_layer(b + 1)
        return carry

    lax.fori_loop(0, edge_blocks - ahead, full_step, 0)
    lax.fori_loop(edge_blocks - ahead, edge_blocks - 1, last_step, 0)
    @pl.when(l >= 0)
    def _():
        add_edges(edge_blocks - 1, group_edges // 2)

    @pl.when(r >= 0)
    def _():
        fine_w, fine_out_w = orders(node_w[0]), orders(centered(out_w[1]))
        near = jnp.concatenate([cext[:BORDER, :], cext[3 * BORDER : EDGE_ROWS, :]], axis=0)
        near_table = dot(near, node_w[1, LAT:, :]).astype(BF16)
        up_w = orders(jnp.concatenate([node_w[1, :LAT, :], near_table], axis=0))
        up_out_w = orders(centered(out_w[2]))
        count = nodes // LAT
        parts = [slice(j * LAT, (j + 1) * LAT) for j in range(count)]
        hs = []
        for j, p in enumerate(parts):
            first = j // 2 * LAT
            agg = acc[first : first + LAT, j % 2 * LAT : (j % 2 + 1) * LAT].T.astype(BF16)
            hs.append(dot(ordered(fine[p, :], agg, j), fine_w[j % 2]))
        cs = [dot(twice(half_silu(0.5 * h)), fine_out_w[j % 2]) for j, h in enumerate(hs)]
        news = [
            (fine[p, :].astype(F32) + scale_rows(c) * gains[1:2, :]).astype(BF16)
            for p, c in zip(parts, cs)
        ]
        for p, new in zip(parts, news):
            mid[p, :] = new
        hs = [
            dot(ordered(new, par_near[p, :], j), up_w[j % 2]) + up_pre[p, :]
            for j, (p, new) in enumerate(zip(parts, news))
        ]
        cs = [dot(twice(half_silu(0.5 * h)), up_out_w[j % 2]) for j, h in enumerate(hs)]
        ups = [split(scale_rows(c) * gains[2:3, :], 1) for c in cs]
        cut = groups // 2 * 2
        sums = dot(par_cols[:, : cut * LAT], jnp.concatenate(ups[:cut], axis=0)) + dot(
            par_cols[:, cut * LAT :], jnp.concatenate(ups[cut:], axis=0)
        )
        sums = sums[:, :LAT] + sums[:, LAT:]
        sums_out[0] = sums[: 2 * BORDER].astype(BF16)
        sums_out[1] = sums[2 * BORDER : EDGE_ROWS].astype(BF16)
        sums_v[...] = sums

    @pl.when(has_lower)
    def _():
        sums_down.start()

    @pl.when(has_upper)
    def _():
        sums_up.start()

    base = cext[EDGE_ROWS:, :]
    h = dot(jnp.concatenate([base, sums_v[EDGE_ROWS:, :].astype(BF16)], axis=1), node_w[2])
    new = scale_rows(dot(twice(half_silu(0.5 * h)), late_out[0])) * gains[3:4, :]
    new = (base.astype(F32) + new).astype(BF16)
    new_inner[...] = new[:inner]
    inner_table = split(dot(new, node_w[3, LAT:, :]), 1)
    for g in range(groups):
        rows = slice(g * TILE, (g + 1) * TILE)
        found = dot(par_inner[rows, :], inner_table)
        down_pre[rows, :] = dot(mid[rows, :], node_w[3, :LAT, :]) + (found[:, :LAT] + found[:, LAT:])
    base_edge[...] = cext[:EDGE_ROWS, :]

    @pl.when(has_lower)
    def _():
        sums_down.wait_send()
        sums_up.wait_recv()

    @pl.when(has_upper)
    def _():
        sums_up.wait_send()
        sums_down.wait_recv()

    total_edge[: 2 * BORDER, :] = (sums_v[: 2 * BORDER, :] + sums_in[0].astype(F32)).astype(BF16)
    total_edge[2 * BORDER :, :] = (sums_v[2 * BORDER : EDGE_ROWS, :] + sums_in[1].astype(F32)).astype(BF16)


def finish(
    mid,
    down_pre,
    par_edge,
    base_edge,
    total_edge,
    new_inner,
    late_w,
    late_out,
    late_gain,
    fine_out,
    coarse_out,
    fine_v,
    coarse_v,
    sem,
):
    nodes, blocks = fine_v.shape[0], coarse_v.shape[0]
    base = base_edge[...]
    h = dot(jnp.concatenate([base, total_edge[...]], axis=1), late_w[0])
    new = scale_rows(dot(twice(half_silu(0.5 * h)), late_out[0])) * late_gain[3:4, :]
    new = (base.astype(F32) + new).astype(BF16)
    coarse_v[:BORDER, :] = new[BORDER : 2 * BORDER]
    coarse_v[blocks - BORDER :, :] = new[2 * BORDER : 3 * BORDER]
    coarse_v[BORDER : blocks - BORDER, :] = new_inner[...]
    copies = [pltpu.make_async_copy(coarse_v, coarse_out, sem.at[nodes // TILE])]
    copies[0].start()
    edge_table = swapped(split(dot(new, late_w[1, LAT:, :]), 1))
    last_w = orders(late_out[1])
    parts = [slice(j * LAT, (j + 1) * LAT) for j in range(nodes // LAT)]
    found = [dot(par_edge[p, :], edge_table[j % 2]) for j, p in enumerate(parts)]
    hs = [down_pre[p, :] + (f[:, :LAT] + f[:, LAT:]) for p, f in zip(parts, found)]
    cs = [dot(twice(half_silu(0.5 * h)), last_w[j % 2]) for j, h in enumerate(hs)]
    for j, c in enumerate(cs):
        p = parts[j]
        new = scale_rows(c) * late_gain[4:5, :]
        fine_v[p, :] = (mid[p, :].astype(F32) + new).astype(BF16)
        if j % 2:
            g = j // 2
            part = pl.ds(g * TILE, TILE)
            copies.append(pltpu.make_async_copy(fine_v.at[part], fine_out.at[part], sem.at[g]))
            copies[-1].start()
    for copy in copies:
        copy.wait()


def body(
    levels,
    fine_nodes,
    coarse_nodes,
    edge_latents,
    senders,
    receivers,
    live_blocks,
    send_list,
    parents,
    edge_weight,
    node_weights,
    out_weights,
    gains,
):
    arrays = (
        fine_nodes,
        coarse_nodes,
        edge_latents,
        senders.reshape(-1, LAT),
        receivers.reshape(-1, LAT),
        live_blocks,
        send_list.reshape(-1, SLOT),
        parents.reshape(-1, LAT),
        edge_weight,
        node_weights,
        out_weights,
        gains,
    )
    nodes, blocks, edges = fine_nodes.shape[0], coarse_nodes.shape[0], edge_latents.shape[0]
    groups, slots = nodes // TILE, send_list.shape[0] // SLOT
    inner = blocks - 2 * BORDER
    hbm = pl.BlockSpec(memory_space=pltpu.HBM)
    vmem = pl.BlockSpec(memory_space=pltpu.VMEM)
    held = [pltpu.VMEM(a.shape, a.dtype) for a in arrays]
    held[5] = pltpu.SMEM((1,), I32)
    edge_blocks = edges // group_edges
    state = pl.pallas_call(
        functools.partial(kernel, levels),
        out_shape=(
            pltpu.VMEM((nodes, LAT), BF16),
            pltpu.VMEM((nodes, LAT), F32),
            pltpu.VMEM((nodes, TILE), BF16),
            pltpu.VMEM((EDGE_ROWS, LAT), BF16),
            pltpu.VMEM((EDGE_ROWS, LAT), BF16),
            pltpu.VMEM((inner, LAT), BF16),
            pltpu.VMEM((2, 2 * LAT, LAT), BF16),
            pltpu.VMEM((2, 2 * LAT, LAT), BF16),
            pltpu.VMEM(gains.shape, F32),
        ),
        in_specs=[hbm] * 12,
        out_specs=(vmem,) * 9,
        scratch_shapes=held
        + [
            pltpu.VMEM((LAT, nodes + slots * SLOT), BF16),
            pltpu.VMEM((2 * LAT, nodes), F32),
            pltpu.VMEM((HALF, lane_tiles * LAT), I32),
            pltpu.VMEM((HALF, nodes), I32),
            pltpu.VMEM((edge_blocks, HALF, group_edges), I32),
            pltpu.VMEM((edge_blocks, LAT, group_edges), BF16),
            pltpu.VMEM((slots, LAT, SLOT), BF16),
            pltpu.VMEM((slots, LAT, SLOT), BF16),
            pltpu.VMEM((2 * TILE, LAT), BF16),
            pltpu.VMEM((nodes, TILE), BF16),
            pltpu.VMEM((nodes, 2 * BORDER), BF16),
            pltpu.VMEM((2 * TILE, nodes), BF16),
            pltpu.VMEM((nodes, LAT), F32),
            pltpu.VMEM((2, 2 * BORDER, LAT), BF16),
            pltpu.VMEM((2, 2 * BORDER, LAT), BF16),
            pltpu.VMEM((2 * TILE, LAT), F32),
            pltpu.VMEM((groups * LAT, TILE), F32),
            pltpu.VMEM((2 * LAT, LAT), BF16),
            pltpu.VMEM((LAT, 2 * LAT), BF16),
            pltpu.VMEM((LAT, LAT), F32),
            pltpu.VMEM((LAT, LAT), F32),
            pltpu.SemaphoreType.DMA((12,)),
            pltpu.SemaphoreType.DMA((7,)),
            pltpu.SemaphoreType.DMA((7,)),
        ],
        compiler_params=pltpu.CompilerParams(
            collective_id=0, has_side_effects=True, vmem_limit_bytes=64_600_000
        ),
        name="graph_step",
    )(*arrays)
    return pl.pallas_call(
        finish,
        out_shape=(
            jax.ShapeDtypeStruct(fine_nodes.shape, BF16),
            jax.ShapeDtypeStruct(coarse_nodes.shape, BF16),
        ),
        in_specs=[vmem] * 9,
        out_specs=(hbm, hbm),
        scratch_shapes=[
            pltpu.VMEM(fine_nodes.shape, BF16),
            pltpu.VMEM(coarse_nodes.shape, BF16),
            pltpu.SemaphoreType.DMA((groups + 1,)),
        ],
        compiler_params=pltpu.CompilerParams(vmem_limit_bytes=16 * 1024 * 1024),
        name="graph_finish",
    )(*state)


def solution(mesh):
    both = ("region", "level")
    in_specs = (
        P(both, None),
        P(both, None),
        P(both, None),
        P(both),
        P(both),
        P(both),
        P(both),
        P(both),
        P(),
        P(),
        P(),
        P(),
    )
    return jax.shard_map(
        functools.partial(body, mesh.shape["level"]),
        mesh=mesh,
        in_specs=in_specs,
        out_specs=(P(both, None), P(both, None)),
        check_vma=False,
    )
```

```python
import functools

import jax
import jax.numpy as jnp
from jax import lax
from jax.experimental import pallas as pl
from jax.experimental.pallas import tpu as pltpu
from jax.sharding import PartitionSpec as P

MESH = pl.DeviceIdType.MESH
F32 = jnp.float32
BF16 = jnp.bfloat16
I32 = jnp.int32
LAT = 128
HALF = LAT // 2
BORDER = 64
EDGE_ROWS = 4 * BORDER
SLOT = 128
norm_eps = 1e-05
group_edges = 1024
sub = group_edges // LAT
TILE = 256
ahead = 3
lane_tiles = 4
top = 16380.0


def dot(a, b, ca=1, cb=0):
    return lax.dot_general(a, b, (((ca,), (cb,)), ((), ())), preferred_element_type=F32)


def half_silu(h):
    return (h * jnp.tanh(h) + h).astype(BF16)


def scale_rows(c):
    return c * lax.rsqrt(jnp.mean(c * c, axis=1, keepdims=True) + norm_eps)


def hot_columns(ids, rows):
    low, high = (ids & (TILE - 1)).astype(F32), ids >> 8
    shape = (TILE, ids.shape[1])
    place = lax.broadcasted_iota(I32, shape, 0).astype(BF16)
    parts = []
    for g in range(rows // TILE):
        mine = jnp.where(high == g, low, -1.0).astype(BF16)
        parts.append(
            jnp.where(place == jnp.broadcast_to(mine, shape), jnp.ones((), BF16), jnp.zeros((), BF16))
        )
    return jnp.concatenate(parts, axis=0)


def split(x, axis):
    high = x.astype(BF16)
    return jnp.concatenate([high, (x - high.astype(F32)).astype(BF16)], axis=axis)


def centered(w):
    wide = w.astype(F32)
    return split(wide - jnp.mean(wide, axis=1, keepdims=True), 0)


def twice(x, axis=1):
    return jnp.concatenate([x, x], axis=axis)


def orders(w):
    return w, jnp.concatenate([w[LAT:], w[:LAT]], axis=0)


def ordered(a, b, part):
    return jnp.concatenate([a, b] if part % 2 == 0 else [b, a], axis=1)


def swapped(w):
    return w, jnp.concatenate([w[:, LAT:], w[:, :LAT]], axis=1)


def kernel(
    levels,
    fine_h,
    coarse_h,
    latents_h,
    senders_h,
    receivers_h,
    live_h,
    send_list_h,
    parents_h,
    edge_w_h,
    node_w_h,
    out_w_h,
    gains_h,
    mid,
    down_pre,
    par_edge,
    base_edge,
    total_edge,
    new_inner,
    late_w,
    late_out,
    late_gain,
    fine,
    coarse,
    latents,
    senders,
    receivers,
    live,
    send_list,
    parents,
    edge_w,
    node_w,
    out_w,
    gains,
    table,
    full,
    sender_q,
    receiver_q,
    own_terms,
    acts,
    outgoing,
    arrived,
    cext,
    par_inner,
    par_near,
    par_cols,
    up_pre,
    sums_out,
    sums_in,
    sums_v,
    up_v,
    acc,
    first_t,
    second_t,
    gain_t,
    scale_t,
    load_sem,
    send_sem,
    recv_sem,
):
    r, l = lax.axis_index("region"), lax.axis_index("level")
    nodes, blocks = fine.shape[0], coarse.shape[0]
    inner = blocks - 2 * BORDER
    ext = blocks + 2 * BORDER
    groups = nodes // TILE
    slots = arrived.shape[0]
    edge_blocks = latents.shape[0] // group_edges
    has_lower, has_upper = l > 0, l < levels - 1
    lower, upper, peer = (r, l - 1), (r, l + 1), (1 - r, l)

    barrier = pltpu.get_barrier_semaphore()
    pl.semaphore_signal(barrier, inc=1, device_id=peer, device_id_type=MESH)

    @pl.when(has_lower)
    def _():
        pl.semaphore_signal(barrier, inc=1, device_id=lower, device_id_type=MESH)

    @pl.when(has_upper)
    def _():
        pl.semaphore_signal(barrier, inc=1, device_id=upper, device_id_type=MESH)

    pairs = [
        (edge_w_h, edge_w),
        (fine_h, fine),
        (send_list_h, send_list),
        (coarse_h, coarse),
        (receivers_h, receivers),
        (senders_h, senders),
        (parents_h, parents),
        (latents_h, latents),
        (out_w_h, out_w),
        (gains_h, gains),
        (node_w_h, node_w),
        (live_h, live),
    ]
    loads = [pltpu.make_async_copy(s, d, load_sem.at[k]) for k, (s, d) in enumerate(pairs)]
    for load in loads:
        load.start()

    def remote(kind, src, dst, device):
        return pltpu.make_async_remote_copy(
            src_ref=src,
            dst_ref=dst,
            send_sem=send_sem.at[kind],
            recv_sem=recv_sem.at[kind],
            device_id=device,
            device_id_type=MESH,
        )

    halo_down = remote(0, outgoing.at[0], arrived.at[1], lower)
    halo_up = remote(1, outgoing.at[1], arrived.at[0], upper)
    halo_peer = remote(2, outgoing.at[3 - r], arrived.at[2 + r], peer)
    coarse_down = remote(3, coarse.at[pl.ds(0, BORDER)], cext.at[pl.ds(3 * BORDER, BORDER)], lower)
    coarse_up = remote(4, coarse.at[pl.ds(blocks - BORDER, BORDER)], cext.at[pl.ds(0, BORDER)], upper)
    sums_down = remote(5, sums_out.at[0], sums_in.at[1], lower)
    sums_up = remote(6, sums_out.at[1], sums_in.at[0], upper)

    loads[0].wait()
    w_both = jnp.concatenate(
        [
            (edge_w[LAT : 2 * LAT, :].astype(F32) * 0.5).T.astype(BF16),
            (edge_w[2 * LAT :, :].astype(F32) * 0.5).T.astype(BF16),
        ],
        axis=0,
    )
    loads[1].wait()
    for g in range(groups):
        both = dot(w_both, fine[g * TILE : (g + 1) * TILE, :], 1, 1)
        full[:, g * TILE : (g + 1) * TILE] = both
        table[:, g * TILE : (g + 1) * TILE] = both[:LAT].astype(BF16)

    loads[2].wait()
    sends = jnp.concatenate([send_list[j : j + 1, :] for j in range(slots)], axis=1)
    picked = dot(table[:, :nodes], hot_columns(sends, nodes)).astype(BF16)
    for j in range(slots):
        outgoing[j] = picked[:, j * SLOT : (j + 1) * SLOT]
    loads[3].wait()

    pl.semaphore_wait(barrier, 1 + has_lower.astype(I32) + has_upper.astype(I32))

    @pl.when(has_lower)
    def _():
        halo_down.start()

    @pl.when(has_upper)
    def _():
        halo_up.start()

    halo_peer.start()

    @pl.when(has_lower)
    def _():
        coarse_down.start()

    @pl.when(has_upper)
    def _():
        coarse_up.start()

    arrived[2 + r] = outgoing[2 + r]
    cext[BORDER : 2 * BORDER, :] = coarse[:BORDER, :]
    cext[2 * BORDER : 3 * BORDER, :] = coarse[blocks - BORDER :, :]
    cext[EDGE_ROWS : EDGE_ROWS + inner, :] = coarse[BORDER : blocks - BORDER, :]
    cext[EDGE_ROWS + inner :, :] = jnp.zeros((cext.shape[0] - EDGE_ROWS - inner, LAT), BF16)

    @pl.when(jnp.logical_not(has_lower))
    def _():
        arrived[0] = jnp.zeros((LAT, SLOT), BF16)
        cext[:BORDER, :] = jnp.zeros((BORDER, LAT), BF16)
        sums_in[0] = jnp.zeros((2 * BORDER, LAT), BF16)

    @pl.when(jnp.logical_not(has_upper))
    def _():
        arrived[1] = jnp.zeros((LAT, SLOT), BF16)
        cext[3 * BORDER : 4 * BORDER, :] = jnp.zeros((BORDER, LAT), BF16)
        sums_in[1] = jnp.zeros((2 * BORDER, LAT), BF16)

    most = jnp.max(jnp.abs(full[...]), axis=1, keepdims=True)
    most = jnp.maximum(jnp.maximum(most[:LAT], most[LAT:]), 1e-30)
    step = most * (1.0 / top)
    scale_t[...] = jnp.broadcast_to(step * (1.0 / 65536.0), (LAT, LAT))
    inverse = top / most

    def pack(start, count, target):
        for t in range(count):
            cols = slice(t * LAT, (t + 1) * LAT)
            q = full[start : start + LAT, cols] * inverse
            low = jnp.round(q[HALF:])
            high = jnp.round(q[:HALF] - low * (1.0 / 65536.0))
            target[:, cols] = high.astype(I32) * 65536 + low.astype(I32)

    pack(0, lane_tiles, sender_q)
    pack(LAT, nodes // LAT, receiver_q)

    loads[4].wait()
    loads[5].wait()
    loads[7].wait()
    first_t[:LAT, :] = (edge_w[:LAT, :].astype(F32) * 0.5).T.astype(BF16)
    scale_all = jnp.concatenate([scale_t[...]] * sub, axis=1)
    skip = lane_tiles * LAT

    def row(ref, b):
        return jnp.concatenate([ref[pl.ds(b * sub + j, 1), :] for j in range(sub)], axis=1)

    def block(b):
        return latents[pl.ds(pl.multiple_of(b * group_edges, group_edges), group_edges), :]

    def gather(b):
        h = dot(first_t[:LAT, :], block(b), 1, 1)
        h = h + dot(table[:, skip:nodes], hot_columns(row(senders, b) - skip, nodes - skip))
        totals = []
        for j in range(sub):

            def look_up(ids, target, x, count):
                low = jnp.broadcast_to(ids & (LAT - 1), (HALF, LAT))
                high = jnp.broadcast_to(ids >> 7, (HALF, LAT))
                for t in range(count):
                    found = jnp.take_along_axis(target[:, t * LAT : (t + 1) * LAT], low, axis=1)
                    x = found if x is None else jnp.where(high == t, found, x)
                return x

            s, t = senders[pl.ds(b * sub + j, 1), :], receivers[pl.ds(b * sub + j, 1), :]
            total = look_up(t, receiver_q, None, nodes // LAT)
            totals.append(total + look_up(s, sender_q, jnp.zeros((HALF, LAT), I32), lane_tiles))
        own = jnp.concatenate(totals, axis=1)
        own = jnp.concatenate([own.astype(F32), (own << 16).astype(F32)], axis=0)
        own_terms[b] = h + own * scale_all


    def gather_step(b, carry):
        gather(b)
        return carry

    lax.fori_loop(0, ahead, gather_step, 0)

    loads[6].wait()
    offset = BORDER - l * blocks
    for j in range(nodes // LAT):
        p = parents[j : j + 1, :] + offset
        p = jnp.where(
            p < 2 * BORDER, p, jnp.where(p < 2 * BORDER + inner, p + 2 * BORDER, p - inner)
        )
        par_cols[:, j * LAT : (j + 1) * LAT] = hot_columns(p, par_cols.shape[0])
        column = jnp.broadcast_to(p.astype(F32), (LAT, LAT)).T
        ids = lax.broadcasted_iota(I32, (LAT, LAT), 1).astype(F32)
        rows = slice(j * LAT, (j + 1) * LAT)
        for k in range(2):
            cols = slice(k * LAT, (k + 1) * LAT)
            par_edge[rows, cols] = jnp.where(ids + float(k * LAT) == column, 1.0, 0.0).astype(BF16)
            par_inner[rows, cols] = jnp.where(
                ids + float(EDGE_ROWS + k * LAT) == column, 1.0, 0.0
            ).astype(BF16)
        near = jnp.where(ids < float(BORDER), ids, ids + float(2 * BORDER))
        par_near[rows, :] = jnp.where(near == column, 1.0, 0.0).astype(BF16)

    for k in range(8, 12):
        loads[k].wait()
    eye = lax.broadcasted_iota(I32, (LAT, LAT), 0) == lax.broadcasted_iota(I32, (LAT, LAT), 1)
    first_t[LAT:, :] = jnp.where(eye, 1.0, 0.0).astype(BF16)
    wide = out_w[0].astype(F32).T
    second_t[...] = split(wide - jnp.mean(wide, axis=0, keepdims=True), 1)
    gain_t[...] = jnp.broadcast_to(gains[0:1, :], (LAT, LAT)).T
    acc[...] = jnp.zeros_like(acc)
    late_w[...] = node_w[2:4]
    late_out[0] = centered(out_w[3])
    late_out[1] = centered(out_w[4])
    late_gain[...] = gains[...]

    none = jnp.zeros((BORDER, LAT), BF16)
    own_edge = jnp.concatenate([none, coarse[:BORDER, :], coarse[blocks - BORDER :, :], none], axis=0)
    edge_table = split(dot(own_edge, node_w[1, LAT:, :]), 1)
    inner_table = split(dot(cext[EDGE_ROWS:, :], node_w[1, LAT:, :]), 1)
    for g in range(groups):
        rows = slice(g * TILE, (g + 1) * TILE)
        found = dot(par_edge[rows, :], edge_table) + dot(par_inner[rows, :], inner_table)
        up_pre[rows, :] = found[:, :LAT] + found[:, LAT:]

    halo_peer.wait()

    @pl.when(has_lower)
    def _():
        halo_down.wait_send()
        halo_up.wait_recv()
        coarse_down.wait_send()
        coarse_up.wait_recv()

    @pl.when(has_upper)
    def _():
        halo_up.wait_send()
        halo_down.wait_recv()
        coarse_up.wait_send()
        coarse_down.wait_recv()

    for j in range(slots):
        table[:, nodes + j * SLOT : nodes + (j + 1) * SLOT] = arrived[j]

    gain_all = jnp.concatenate([gain_t[...]] * sub, axis=1)

    def hidden_layer(b):
        hot = hot_columns(row(senders, b) - nodes, slots * SLOT)
        acts[b] = half_silu(own_terms[b] + dot(table[:, nodes:], hot))

    def add_edges(b, cut=group_edges):
        lat = dot(first_t[LAT:, :], block(b), 1, 1)
        c = dot(second_t[...], twice(acts[b], 0))
        spread = lax.rsqrt(jnp.mean(c * c, axis=0, keepdims=True) + norm_eps)
        updated = (lat + c * spread * gain_all).astype(BF16)
        ids = row(receivers, b)
        position = b * group_edges + lax.broadcasted_iota(I32, (1, group_edges), 1)
        target = jnp.where(position < live[0] * 128, ids >> 8, groups)
        masks = [jnp.where(target == g, 1.0, 0.0).astype(BF16) for g in range(groups)]
        hot = hot_columns(ids & (TILE - 1), TILE)

        def summed(cols):
            part = updated[:, cols]
            masked = [part * jnp.broadcast_to(mask[:, cols], part.shape) for mask in masks]
            return dot(jnp.concatenate(masked, axis=0), hot[:, cols], 1, 1)

        total = summed(slice(0, cut))
        if cut < group_edges:
            total = total + summed(slice(cut, group_edges))
        acc[...] += total

    hidden_layer(0)

    def full_step(b, carry):
        add_edges(b)
        hidden_layer(b + 1)
        gather(b + ahead)
        return carry

    def last_step(b, carry):
        add_edges(b)
        hidden_layer(b + 1)
        return carry

    lax.fori_loop(0, edge_blocks - ahead, full_step, 0)
    lax.fori_loop(edge_blocks - ahead, edge_blocks - 1, last_step, 0)
    @pl.when(l >= 0)
    def _():
        add_edges(edge_blocks - 1, group_edges // 2)

    @pl.when(r >= 0)
    def _():
        fine_w, fine_out_w = orders(node_w[0]), orders(centered(out_w[1]))
        near = jnp.concatenate([cext[:BORDER, :], cext[3 * BORDER : EDGE_ROWS, :]], axis=0)
        near_table = dot(near, node_w[1, LAT:, :]).astype(BF16)
        up_w = orders(jnp.concatenate([node_w[1, :LAT, :], near_table], axis=0))
        up_out_w = orders(centered(out_w[2]))
        count = nodes // LAT
        parts = [slice(j * LAT, (j + 1) * LAT) for j in range(count)]
        hs = []
        for j, p in enumerate(parts):
            first = j // 2 * LAT
            agg = acc[first : first + LAT, j % 2 * LAT : (j % 2 + 1) * LAT].T.astype(BF16)
            hs.append(dot(ordered(fine[p, :], agg, j), fine_w[j % 2]))
        cs = [dot(twice(half_silu(0.5 * h)), fine_out_w[j % 2]) for j, h in enumerate(hs)]
        news = [
            (fine[p, :].astype(F32) + scale_rows(c) * gains[1:2, :]).astype(BF16)
            for p, c in zip(parts, cs)
        ]
        for p, new in zip(parts, news):
            mid[p, :] = new
        hs = [
            dot(ordered(new, par_near[p, :], j), up_w[j % 2]) + up_pre[p, :]
            for j, (p, new) in enumerate(zip(parts, news))
        ]
        cs = [dot(twice(half_silu(0.5 * h)), up_out_w[j % 2]) for j, h in enumerate(hs)]
        ups = [split(scale_rows(c) * gains[2:3, :], 1) for c in cs]
        for p, up in zip(parts, ups):
            up_v[p, :] = up
        cut = groups // 2 * 2
        sums = dot(par_cols[:EDGE_ROWS, : cut * LAT], jnp.concatenate(ups[:cut], axis=0)) + dot(
            par_cols[:EDGE_ROWS, cut * LAT :], jnp.concatenate(ups[cut:], axis=0)
        )
        sums = sums[:, :LAT] + sums[:, LAT:]
        sums_out[0] = sums[: 2 * BORDER].astype(BF16)
        sums_out[1] = sums[2 * BORDER :].astype(BF16)
        sums_v[...] = sums

    @pl.when(has_lower)
    def _():
        sums_down.start()

    @pl.when(has_upper)
    def _():
        sums_up.start()

    base = cext[EDGE_ROWS:, :]
    sums = dot(par_cols[EDGE_ROWS:, :], up_v[...])
    sums = (sums[:, :LAT] + sums[:, LAT:]).astype(BF16)
    h = dot(jnp.concatenate([base, sums], axis=1), node_w[2])
    new = scale_rows(dot(twice(half_silu(0.5 * h)), late_out[0])) * gains[3:4, :]
    new = (base.astype(F32) + new).astype(BF16)
    new_inner[...] = new[:inner]
    inner_table = split(dot(new, node_w[3, LAT:, :]), 1)
    for g in range(groups):
        rows = slice(g * TILE, (g + 1) * TILE)
        found = dot(par_inner[rows, :], inner_table)
        down_pre[rows, :] = dot(mid[rows, :], node_w[3, :LAT, :]) + (found[:, :LAT] + found[:, LAT:])
    base_edge[...] = cext[:EDGE_ROWS, :]

    @pl.when(has_lower)
    def _():
        sums_down.wait_send()
        sums_up.wait_recv()

    @pl.when(has_upper)
    def _():
        sums_up.wait_send()
        sums_down.wait_recv()

    total_edge[: 2 * BORDER, :] = (sums_v[: 2 * BORDER, :] + sums_in[0].astype(F32)).astype(BF16)
    total_edge[2 * BORDER :, :] = (sums_v[2 * BORDER : EDGE_ROWS, :] + sums_in[1].astype(F32)).astype(BF16)


def finish(
    mid,
    down_pre,
    par_edge,
    base_edge,
    total_edge,
    new_inner,
    late_w,
    late_out,
    late_gain,
    fine_out,
    coarse_out,
    fine_v,
    coarse_v,
    sem,
):
    nodes, blocks = fine_v.shape[0], coarse_v.shape[0]
    base = base_edge[...]
    h = dot(jnp.concatenate([base, total_edge[...]], axis=1), late_w[0])
    new = scale_rows(dot(twice(half_silu(0.5 * h)), late_out[0])) * late_gain[3:4, :]
    new = (base.astype(F32) + new).astype(BF16)
    coarse_v[:BORDER, :] = new[BORDER : 2 * BORDER]
    coarse_v[blocks - BORDER :, :] = new[2 * BORDER : 3 * BORDER]
    coarse_v[BORDER : blocks - BORDER, :] = new_inner[...]
    copies = [pltpu.make_async_copy(coarse_v, coarse_out, sem.at[nodes // TILE])]
    copies[0].start()
    edge_table = swapped(split(dot(new, late_w[1, LAT:, :]), 1))
    last_w = orders(late_out[1])
    parts = [slice(j * LAT, (j + 1) * LAT) for j in range(nodes // LAT)]
    found = [dot(par_edge[p, :], edge_table[j % 2]) for j, p in enumerate(parts)]
    hs = [down_pre[p, :] + (f[:, :LAT] + f[:, LAT:]) for p, f in zip(parts, found)]
    cs = [dot(twice(half_silu(0.5 * h)), last_w[j % 2]) for j, h in enumerate(hs)]
    for j, c in enumerate(cs):
        p = parts[j]
        new = scale_rows(c) * late_gain[4:5, :]
        fine_v[p, :] = (mid[p, :].astype(F32) + new).astype(BF16)
        if j % 2:
            g = j // 2
            part = pl.ds(g * TILE, TILE)
            copies.append(pltpu.make_async_copy(fine_v.at[part], fine_out.at[part], sem.at[g]))
            copies[-1].start()
    for copy in copies:
        copy.wait()


def body(
    levels,
    fine_nodes,
    coarse_nodes,
    edge_latents,
    senders,
    receivers,
    live_blocks,
    send_list,
    parents,
    edge_weight,
    node_weights,
    out_weights,
    gains,
):
    arrays = (
        fine_nodes,
        coarse_nodes,
        edge_latents,
        senders.reshape(-1, LAT),
        receivers.reshape(-1, LAT),
        live_blocks,
        send_list.reshape(-1, SLOT),
        parents.reshape(-1, LAT),
        edge_weight,
        node_weights,
        out_weights,
        gains,
    )
    nodes, blocks, edges = fine_nodes.shape[0], coarse_nodes.shape[0], edge_latents.shape[0]
    groups, slots = nodes // TILE, send_list.shape[0] // SLOT
    inner = blocks - 2 * BORDER
    hbm = pl.BlockSpec(memory_space=pltpu.HBM)
    vmem = pl.BlockSpec(memory_space=pltpu.VMEM)
    held = [pltpu.VMEM(a.shape, a.dtype) for a in arrays]
    held[5] = pltpu.SMEM((1,), I32)
    edge_blocks = edges // group_edges
    state = pl.pallas_call(
        functools.partial(kernel, levels),
        out_shape=(
            pltpu.VMEM((nodes, LAT), BF16),
            pltpu.VMEM((nodes, LAT), F32),
            pltpu.VMEM((nodes, TILE), BF16),
            pltpu.VMEM((EDGE_ROWS, LAT), BF16),
            pltpu.VMEM((EDGE_ROWS, LAT), BF16),
            pltpu.VMEM((inner, LAT), BF16),
            pltpu.VMEM((2, 2 * LAT, LAT), BF16),
            pltpu.VMEM((2, 2 * LAT, LAT), BF16),
            pltpu.VMEM(gains.shape, F32),
        ),
        in_specs=[hbm] * 12,
        out_specs=(vmem,) * 9,
        scratch_shapes=held
        + [
            pltpu.VMEM((LAT, nodes + slots * SLOT), BF16),
            pltpu.VMEM((2 * LAT, nodes), F32),
            pltpu.VMEM((HALF, lane_tiles * LAT), I32),
            pltpu.VMEM((HALF, nodes), I32),
            pltpu.VMEM((edge_blocks, LAT, group_edges), F32),
            pltpu.VMEM((edge_blocks, LAT, group_edges), BF16),
            pltpu.VMEM((slots, LAT, SLOT), BF16),
            pltpu.VMEM((slots, LAT, SLOT), BF16),
            pltpu.VMEM((2 * TILE, LAT), BF16),
            pltpu.VMEM((nodes, TILE), BF16),
            pltpu.VMEM((nodes, 2 * BORDER), BF16),
            pltpu.VMEM((2 * TILE, nodes), BF16),
            pltpu.VMEM((nodes, LAT), F32),
            pltpu.VMEM((2, 2 * BORDER, LAT), BF16),
            pltpu.VMEM((2, 2 * BORDER, LAT), BF16),
            pltpu.VMEM((EDGE_ROWS, LAT), F32),
            pltpu.VMEM((nodes, 2 * LAT), BF16),
            pltpu.VMEM((groups * LAT, TILE), F32),
            pltpu.VMEM((2 * LAT, LAT), BF16),
            pltpu.VMEM((LAT, 2 * LAT), BF16),
            pltpu.VMEM((LAT, LAT), F32),
            pltpu.VMEM((LAT, LAT), F32),
            pltpu.SemaphoreType.DMA((12,)),
            pltpu.SemaphoreType.DMA((7,)),
            pltpu.SemaphoreType.DMA((7,)),
        ],
        compiler_params=pltpu.CompilerParams(
            collective_id=0, has_side_effects=True, vmem_limit_bytes=64_600_000
        ),
        name="graph_step",
    )(*arrays)
    return pl.pallas_call(
        finish,
        out_shape=(
            jax.ShapeDtypeStruct(fine_nodes.shape, BF16),
            jax.ShapeDtypeStruct(coarse_nodes.shape, BF16),
        ),
        in_specs=[vmem] * 9,
        out_specs=(hbm, hbm),
        scratch_shapes=[
            pltpu.VMEM(fine_nodes.shape, BF16),
            pltpu.VMEM(coarse_nodes.shape, BF16),
            pltpu.SemaphoreType.DMA((groups + 1,)),
        ],
        compiler_params=pltpu.CompilerParams(vmem_limit_bytes=16 * 1024 * 1024),
        name="graph_finish",
    )(*state)


def solution(mesh):
    both = ("region", "level")
    in_specs = (
        P(both, None),
        P(both, None),
        P(both, None),
        P(both),
        P(both),
        P(both),
        P(both),
        P(both),
        P(),
        P(),
        P(),
        P(),
    )
    return jax.shard_map(
        functools.partial(body, mesh.shape["level"]),
        mesh=mesh,
        in_specs=in_specs,
        out_specs=(P(both, None), P(both, None)),
        check_vma=False,
    )
```

```python
import functools

import jax
import jax.numpy as jnp
from jax import lax
from jax.experimental import pallas as pl
from jax.experimental.pallas import tpu as pltpu
from jax.sharding import PartitionSpec as P

MESH = pl.DeviceIdType.MESH
F32 = jnp.float32
BF16 = jnp.bfloat16
I32 = jnp.int32
LAT = 128
HALF = LAT // 2
BORDER = 64
EDGE_ROWS = 4 * BORDER
SLOT = 128
norm_eps = 1e-05
group_edges = 1024
sub = group_edges // LAT
TILE = 256
ahead = 5
lane_tiles = 0
top = 16380.0


def dot(a, b, ca=1, cb=0):
    return lax.dot_general(a, b, (((ca,), (cb,)), ((), ())), preferred_element_type=F32)


def half_silu(h):
    return (h * jnp.tanh(h) + h).astype(BF16)


def scale_rows(c):
    return c * lax.rsqrt(jnp.mean(c * c, axis=1, keepdims=True) + norm_eps)


def hot_columns(ids, rows):
    low, high = (ids & (TILE - 1)).astype(F32), ids >> 8
    shape = (TILE, ids.shape[1])
    place = lax.broadcasted_iota(I32, shape, 0).astype(BF16)
    parts = []
    for g in range(rows // TILE):
        mine = jnp.where(high == g, low, -1.0).astype(BF16)
        parts.append(
            jnp.where(place == jnp.broadcast_to(mine, shape), jnp.ones((), BF16), jnp.zeros((), BF16))
        )
    return jnp.concatenate(parts, axis=0)


def split(x, axis):
    high = x.astype(BF16)
    return jnp.concatenate([high, (x - high.astype(F32)).astype(BF16)], axis=axis)


def centered(w):
    wide = w.astype(F32)
    return split(wide - jnp.mean(wide, axis=1, keepdims=True), 0)


def twice(x, axis=1):
    return jnp.concatenate([x, x], axis=axis)


def orders(w):
    return w, jnp.concatenate([w[LAT:], w[:LAT]], axis=0)


def ordered(a, b, part):
    return jnp.concatenate([a, b] if part % 2 == 0 else [b, a], axis=1)


def swapped(w):
    return w, jnp.concatenate([w[:, LAT:], w[:, :LAT]], axis=1)


def kernel(
    levels,
    fine_h,
    coarse_h,
    latents_h,
    senders_h,
    receivers_h,
    live_h,
    send_list_h,
    parents_h,
    edge_w_h,
    node_w_h,
    out_w_h,
    gains_h,
    mid,
    down_pre,
    par_edge,
    base_edge,
    total_edge,
    new_inner,
    late_w,
    late_out,
    late_gain,
    fine,
    coarse,
    latents,
    senders,
    receivers,
    live,
    send_list,
    parents,
    edge_w,
    node_w,
    out_w,
    gains,
    table,
    full,
    sender_q,
    receiver_q,
    own_terms,
    acts,
    outgoing,
    arrived,
    cext,
    par_inner,
    par_near,
    par_cols,
    up_pre,
    sums_out,
    sums_in,
    sums_v,
    up_v,
    acc,
    first_t,
    second_t,
    gain_t,
    scale_t,
    load_sem,
    send_sem,
    recv_sem,
):
    r, l = lax.axis_index("region"), lax.axis_index("level")
    nodes, blocks = fine.shape[0], coarse.shape[0]
    inner = blocks - 2 * BORDER
    ext = blocks + 2 * BORDER
    groups = nodes // TILE
    slots = arrived.shape[0]
    edge_blocks = latents.shape[0] // group_edges
    has_lower, has_upper = l > 0, l < levels - 1
    lower, upper, peer = (r, l - 1), (r, l + 1), (1 - r, l)

    barrier = pltpu.get_barrier_semaphore()
    pl.semaphore_signal(barrier, inc=1, device_id=peer, device_id_type=MESH)

    @pl.when(has_lower)
    def _():
        pl.semaphore_signal(barrier, inc=1, device_id=lower, device_id_type=MESH)

    @pl.when(has_upper)
    def _():
        pl.semaphore_signal(barrier, inc=1, device_id=upper, device_id_type=MESH)

    pairs = [
        (edge_w_h, edge_w),
        (fine_h, fine),
        (send_list_h, send_list),
        (coarse_h, coarse),
        (receivers_h, receivers),
        (senders_h, senders),
        (parents_h, parents),
        (latents_h, latents),
        (out_w_h, out_w),
        (gains_h, gains),
        (node_w_h, node_w),
        (live_h, live),
    ]
    loads = [pltpu.make_async_copy(s, d, load_sem.at[k]) for k, (s, d) in enumerate(pairs)]
    for load in loads:
        load.start()

    def remote(kind, src, dst, device):
        return pltpu.make_async_remote_copy(
            src_ref=src,
            dst_ref=dst,
            send_sem=send_sem.at[kind],
            recv_sem=recv_sem.at[kind],
            device_id=device,
            device_id_type=MESH,
        )

    halo_down = remote(0, outgoing.at[0], arrived.at[1], lower)
    halo_up = remote(1, outgoing.at[1], arrived.at[0], upper)
    halo_peer = remote(2, outgoing.at[3 - r], arrived.at[2 + r], peer)
    coarse_down = remote(3, coarse.at[pl.ds(0, BORDER)], cext.at[pl.ds(3 * BORDER, BORDER)], lower)
    coarse_up = remote(4, coarse.at[pl.ds(blocks - BORDER, BORDER)], cext.at[pl.ds(0, BORDER)], upper)
    sums_down = remote(5, sums_out.at[0], sums_in.at[1], lower)
    sums_up = remote(6, sums_out.at[1], sums_in.at[0], upper)

    loads[0].wait()
    w_both = jnp.concatenate(
        [
            (edge_w[LAT : 2 * LAT, :].astype(F32) * 0.5).T.astype(BF16),
            (edge_w[2 * LAT :, :].astype(F32) * 0.5).T.astype(BF16),
        ],
        axis=0,
    )
    loads[1].wait()
    for g in range(groups):
        both = dot(w_both, fine[g * TILE : (g + 1) * TILE, :], 1, 1)
        full[:, g * TILE : (g + 1) * TILE] = both
        table[:, g * TILE : (g + 1) * TILE] = both[:LAT].astype(BF16)

    loads[2].wait()
    sends = jnp.concatenate([send_list[j : j + 1, :] for j in range(slots)], axis=1)
    picked = dot(table[:, :nodes], hot_columns(sends, nodes)).astype(BF16)
    for j in range(slots):
        outgoing[j] = picked[:, j * SLOT : (j + 1) * SLOT]
    loads[3].wait()

    pl.semaphore_wait(barrier, 1 + has_lower.astype(I32) + has_upper.astype(I32))

    @pl.when(has_lower)
    def _():
        halo_down.start()

    @pl.when(has_upper)
    def _():
        halo_up.start()

    halo_peer.start()

    @pl.when(has_lower)
    def _():
        coarse_down.start()

    @pl.when(has_upper)
    def _():
        coarse_up.start()

    arrived[2 + r] = outgoing[2 + r]
    cext[BORDER : 2 * BORDER, :] = coarse[:BORDER, :]
    cext[2 * BORDER : 3 * BORDER, :] = coarse[blocks - BORDER :, :]
    cext[EDGE_ROWS : EDGE_ROWS + inner, :] = coarse[BORDER : blocks - BORDER, :]
    cext[EDGE_ROWS + inner :, :] = jnp.zeros((cext.shape[0] - EDGE_ROWS - inner, LAT), BF16)

    @pl.when(jnp.logical_not(has_lower))
    def _():
        arrived[0] = jnp.zeros((LAT, SLOT), BF16)
        cext[:BORDER, :] = jnp.zeros((BORDER, LAT), BF16)
        sums_in[0] = jnp.zeros((2 * BORDER, LAT), BF16)

    @pl.when(jnp.logical_not(has_upper))
    def _():
        arrived[1] = jnp.zeros((LAT, SLOT), BF16)
        cext[3 * BORDER : 4 * BORDER, :] = jnp.zeros((BORDER, LAT), BF16)
        sums_in[1] = jnp.zeros((2 * BORDER, LAT), BF16)

    most = jnp.max(jnp.abs(full[...]), axis=1, keepdims=True)
    most = jnp.maximum(jnp.maximum(most[:LAT], most[LAT:]), 1e-30)
    step = most * (1.0 / top)
    scale_t[...] = jnp.broadcast_to(step * (1.0 / 65536.0), (LAT, LAT))
    inverse = top / most

    def pack(start, count, target):
        for t in range(count):
            cols = slice(t * LAT, (t + 1) * LAT)
            q = full[start : start + LAT, cols] * inverse
            low = jnp.round(q[HALF:])
            high = jnp.round(q[:HALF] - low * (1.0 / 65536.0))
            target[:, cols] = high.astype(I32) * 65536 + low.astype(I32)

    pack(0, lane_tiles, sender_q)
    pack(LAT, nodes // LAT, receiver_q)

    loads[4].wait()
    loads[5].wait()
    loads[7].wait()
    first_t[:LAT, :] = (edge_w[:LAT, :].astype(F32) * 0.5).T.astype(BF16)
    scale_all = jnp.concatenate([scale_t[...]] * sub, axis=1)
    skip = lane_tiles * LAT

    def row(ref, b):
        return jnp.concatenate([ref[pl.ds(b * sub + j, 1), :] for j in range(sub)], axis=1)

    def block(b):
        return latents[pl.ds(pl.multiple_of(b * group_edges, group_edges), group_edges), :]

    def gather(b):
        h = dot(first_t[:LAT, :], block(b), 1, 1)
        h = h + dot(table[:, skip:nodes], hot_columns(row(senders, b) - skip, nodes - skip))
        totals = []
        for j in range(sub):

            def look_up(ids, target, x, count):
                low = jnp.broadcast_to(ids & (LAT - 1), (HALF, LAT))
                high = jnp.broadcast_to(ids >> 7, (HALF, LAT))
                for t in range(count):
                    found = jnp.take_along_axis(target[:, t * LAT : (t + 1) * LAT], low, axis=1)
                    x = found if x is None else jnp.where(high == t, found, x)
                return x

            s, t = senders[pl.ds(b * sub + j, 1), :], receivers[pl.ds(b * sub + j, 1), :]
            total = look_up(t, receiver_q, None, nodes // LAT)
            if lane_tiles:
                total = total + look_up(s, sender_q, jnp.zeros((HALF, LAT), I32), lane_tiles)
            totals.append(total)
        own = jnp.concatenate(totals, axis=1)
        own = jnp.concatenate([own.astype(F32), (own << 16).astype(F32)], axis=0)
        own_terms[b] = h + own * scale_all


    def gather_step(b, carry):
        gather(b)
        return carry

    lax.fori_loop(0, ahead, gather_step, 0)

    loads[6].wait()
    offset = BORDER - l * blocks
    for j in range(nodes // LAT):
        p = parents[j : j + 1, :] + offset
        p = jnp.where(
            p < 2 * BORDER, p, jnp.where(p < 2 * BORDER + inner, p + 2 * BORDER, p - inner)
        )
        par_cols[:, j * LAT : (j + 1) * LAT] = hot_columns(p, par_cols.shape[0])
        column = jnp.broadcast_to(p.astype(F32), (LAT, LAT)).T
        ids = lax.broadcasted_iota(I32, (LAT, LAT), 1).astype(F32)
        rows = slice(j * LAT, (j + 1) * LAT)
        for k in range(2):
            cols = slice(k * LAT, (k + 1) * LAT)
            par_edge[rows, cols] = jnp.where(ids + float(k * LAT) == column, 1.0, 0.0).astype(BF16)
            par_inner[rows, cols] = jnp.where(
                ids + float(EDGE_ROWS + k * LAT) == column, 1.0, 0.0
            ).astype(BF16)
        near = jnp.where(ids < float(BORDER), ids, ids + float(2 * BORDER))
        par_near[rows, :] = jnp.where(near == column, 1.0, 0.0).astype(BF16)

    for k in range(8, 12):
        loads[k].wait()
    eye = lax.broadcasted_iota(I32, (LAT, LAT), 0) == lax.broadcasted_iota(I32, (LAT, LAT), 1)
    first_t[LAT:, :] = jnp.where(eye, 1.0, 0.0).astype(BF16)
    wide = out_w[0].astype(F32).T
    second_t[...] = split(wide - jnp.mean(wide, axis=0, keepdims=True), 1)
    gain_t[...] = jnp.broadcast_to(gains[0:1, :], (LAT, LAT)).T
    acc[...] = jnp.zeros_like(acc)
    late_w[...] = node_w[2:4]
    late_out[0] = centered(out_w[3])
    late_out[1] = centered(out_w[4])
    late_gain[...] = gains[...]

    none = jnp.zeros((BORDER, LAT), BF16)
    own_edge = jnp.concatenate([none, coarse[:BORDER, :], coarse[blocks - BORDER :, :], none], axis=0)
    edge_table = split(dot(own_edge, node_w[1, LAT:, :]), 1)
    inner_table = split(dot(cext[EDGE_ROWS:, :], node_w[1, LAT:, :]), 1)
    for g in range(groups):
        rows = slice(g * TILE, (g + 1) * TILE)
        found = dot(par_edge[rows, :], edge_table) + dot(par_inner[rows, :], inner_table)
        up_pre[rows, :] = found[:, :LAT] + found[:, LAT:]

    halo_peer.wait()

    @pl.when(has_lower)
    def _():
        halo_down.wait_send()
        halo_up.wait_recv()
        coarse_down.wait_send()
        coarse_up.wait_recv()

    @pl.when(has_upper)
    def _():
        halo_up.wait_send()
        halo_down.wait_recv()
        coarse_up.wait_send()
        coarse_down.wait_recv()

    for j in range(slots):
        table[:, nodes + j * SLOT : nodes + (j + 1) * SLOT] = arrived[j]

    gain_all = jnp.concatenate([gain_t[...]] * sub, axis=1)

    def hidden_layer(b):
        hot = hot_columns(row(senders, b) - nodes, slots * SLOT)
        acts[b] = half_silu(own_terms[b] + dot(table[:, nodes:], hot))

    def add_edges(b, cut=group_edges):
        lat = dot(first_t[LAT:, :], block(b), 1, 1)
        c = dot(second_t[...], twice(acts[b], 0))
        spread = lax.rsqrt(jnp.mean(c * c, axis=0, keepdims=True) + norm_eps)
        updated = (lat + c * spread * gain_all).astype(BF16)
        ids = row(receivers, b)
        position = b * group_edges + lax.broadcasted_iota(I32, (1, group_edges), 1)
        target = jnp.where(position < live[0] * 128, ids >> 8, groups)
        masks = [jnp.where(target == g, 1.0, 0.0).astype(BF16) for g in range(groups)]
        hot = hot_columns(ids & (TILE - 1), TILE)

        def summed(cols):
            part = updated[:, cols]
            masked = [part * jnp.broadcast_to(mask[:, cols], part.shape) for mask in masks]
            return dot(jnp.concatenate(masked, axis=0), hot[:, cols], 1, 1)

        total = summed(slice(0, cut))
        if cut < group_edges:
            total = total + summed(slice(cut, group_edges))
        acc[...] += total

    hidden_layer(0)

    def full_step(b, carry):
        add_edges(b)
        hidden_layer(b + 1)
        gather(b + ahead)
        return carry

    def last_step(b, carry):
        add_edges(b)
        hidden_layer(b + 1)
        return carry

    lax.fori_loop(0, edge_blocks - ahead, full_step, 0)
    lax.fori_loop(edge_blocks - ahead, edge_blocks - 1, last_step, 0)
    @pl.when(l >= 0)
    def _():
        add_edges(edge_blocks - 1, group_edges // 2)

    @pl.when(r >= 0)
    def _():
        fine_w, fine_out_w = orders(node_w[0]), orders(centered(out_w[1]))
        near = jnp.concatenate([cext[:BORDER, :], cext[3 * BORDER : EDGE_ROWS, :]], axis=0)
        near_table = dot(near, node_w[1, LAT:, :]).astype(BF16)
        up_w = orders(jnp.concatenate([node_w[1, :LAT, :], near_table], axis=0))
        up_out_w = orders(centered(out_w[2]))
        count = nodes // LAT
        parts = [slice(j * LAT, (j + 1) * LAT) for j in range(count)]
        hs = []
        for j, p in enumerate(parts):
            first = j // 2 * LAT
            agg = acc[first : first + LAT, j % 2 * LAT : (j % 2 + 1) * LAT].T.astype(BF16)
            hs.append(dot(ordered(fine[p, :], agg, j), fine_w[j % 2]))
        cs = [dot(twice(half_silu(0.5 * h)), fine_out_w[j % 2]) for j, h in enumerate(hs)]
        news = [
            (fine[p, :].astype(F32) + scale_rows(c) * gains[1:2, :]).astype(BF16)
            for p, c in zip(parts, cs)
        ]
        for p, new in zip(parts, news):
            mid[p, :] = new
        hs = [
            dot(ordered(new, par_near[p, :], j), up_w[j % 2]) + up_pre[p, :]
            for j, (p, new) in enumerate(zip(parts, news))
        ]
        cs = [dot(twice(half_silu(0.5 * h)), up_out_w[j % 2]) for j, h in enumerate(hs)]
        ups = [split(scale_rows(c) * gains[2:3, :], 1) for c in cs]
        for p, up in zip(parts, ups):
            up_v[p, :] = up
        cut = groups // 2 * 2
        sums = dot(par_cols[:EDGE_ROWS, : cut * LAT], jnp.concatenate(ups[:cut], axis=0)) + dot(
            par_cols[:EDGE_ROWS, cut * LAT :], jnp.concatenate(ups[cut:], axis=0)
        )
        sums = sums[:, :LAT] + sums[:, LAT:]
        sums_out[0] = sums[: 2 * BORDER].astype(BF16)
        sums_out[1] = sums[2 * BORDER :].astype(BF16)
        sums_v[...] = sums

    @pl.when(has_lower)
    def _():
        sums_down.start()

    @pl.when(has_upper)
    def _():
        sums_up.start()

    base = cext[EDGE_ROWS:, :]
    sums = dot(par_cols[EDGE_ROWS:, :], up_v[...])
    sums = (sums[:, :LAT] + sums[:, LAT:]).astype(BF16)
    h = dot(jnp.concatenate([base, sums], axis=1), node_w[2])
    new = scale_rows(dot(twice(half_silu(0.5 * h)), late_out[0])) * gains[3:4, :]
    new = (base.astype(F32) + new).astype(BF16)
    new_inner[...] = new[:inner]
    inner_table = split(dot(new, node_w[3, LAT:, :]), 1)
    for g in range(groups):
        rows = slice(g * TILE, (g + 1) * TILE)
        found = dot(par_inner[rows, :], inner_table)
        down_pre[rows, :] = dot(mid[rows, :], node_w[3, :LAT, :]) + (found[:, :LAT] + found[:, LAT:])
    base_edge[...] = cext[:EDGE_ROWS, :]

    @pl.when(has_lower)
    def _():
        sums_down.wait_send()
        sums_up.wait_recv()

    @pl.when(has_upper)
    def _():
        sums_up.wait_send()
        sums_down.wait_recv()

    total_edge[: 2 * BORDER, :] = (sums_v[: 2 * BORDER, :] + sums_in[0].astype(F32)).astype(BF16)
    total_edge[2 * BORDER :, :] = (sums_v[2 * BORDER : EDGE_ROWS, :] + sums_in[1].astype(F32)).astype(BF16)


def finish(
    mid,
    down_pre,
    par_edge,
    base_edge,
    total_edge,
    new_inner,
    late_w,
    late_out,
    late_gain,
    fine_out,
    coarse_out,
    fine_v,
    coarse_v,
    sem,
):
    nodes, blocks = fine_v.shape[0], coarse_v.shape[0]
    base = base_edge[...]
    h = dot(jnp.concatenate([base, total_edge[...]], axis=1), late_w[0])
    new = scale_rows(dot(twice(half_silu(0.5 * h)), late_out[0])) * late_gain[3:4, :]
    new = (base.astype(F32) + new).astype(BF16)
    coarse_v[:BORDER, :] = new[BORDER : 2 * BORDER]
    coarse_v[blocks - BORDER :, :] = new[2 * BORDER : 3 * BORDER]
    coarse_v[BORDER : blocks - BORDER, :] = new_inner[...]
    copies = [pltpu.make_async_copy(coarse_v, coarse_out, sem.at[nodes // TILE])]
    copies[0].start()
    edge_table = swapped(split(dot(new, late_w[1, LAT:, :]), 1))
    last_w = orders(late_out[1])
    parts = [slice(j * LAT, (j + 1) * LAT) for j in range(nodes // LAT)]
    found = [dot(par_edge[p, :], edge_table[j % 2]) for j, p in enumerate(parts)]
    hs = [down_pre[p, :] + (f[:, :LAT] + f[:, LAT:]) for p, f in zip(parts, found)]
    cs = [dot(twice(half_silu(0.5 * h)), last_w[j % 2]) for j, h in enumerate(hs)]
    for j, c in enumerate(cs):
        p = parts[j]
        new = scale_rows(c) * late_gain[4:5, :]
        fine_v[p, :] = (mid[p, :].astype(F32) + new).astype(BF16)
        if j % 2:
            g = j // 2
            part = pl.ds(g * TILE, TILE)
            copies.append(pltpu.make_async_copy(fine_v.at[part], fine_out.at[part], sem.at[g]))
            copies[-1].start()
    for copy in copies:
        copy.wait()


def body(
    levels,
    fine_nodes,
    coarse_nodes,
    edge_latents,
    senders,
    receivers,
    live_blocks,
    send_list,
    parents,
    edge_weight,
    node_weights,
    out_weights,
    gains,
):
    arrays = (
        fine_nodes,
        coarse_nodes,
        edge_latents,
        senders.reshape(-1, LAT),
        receivers.reshape(-1, LAT),
        live_blocks,
        send_list.reshape(-1, SLOT),
        parents.reshape(-1, LAT),
        edge_weight,
        node_weights,
        out_weights,
        gains,
    )
    nodes, blocks, edges = fine_nodes.shape[0], coarse_nodes.shape[0], edge_latents.shape[0]
    groups, slots = nodes // TILE, send_list.shape[0] // SLOT
    inner = blocks - 2 * BORDER
    hbm = pl.BlockSpec(memory_space=pltpu.HBM)
    vmem = pl.BlockSpec(memory_space=pltpu.VMEM)
    held = [pltpu.VMEM(a.shape, a.dtype) for a in arrays]
    held[5] = pltpu.SMEM((1,), I32)
    edge_blocks = edges // group_edges
    state = pl.pallas_call(
        functools.partial(kernel, levels),
        out_shape=(
            pltpu.VMEM((nodes, LAT), BF16),
            pltpu.VMEM((nodes, LAT), F32),
            pltpu.VMEM((nodes, TILE), BF16),
            pltpu.VMEM((EDGE_ROWS, LAT), BF16),
            pltpu.VMEM((EDGE_ROWS, LAT), BF16),
            pltpu.VMEM((inner, LAT), BF16),
            pltpu.VMEM((2, 2 * LAT, LAT), BF16),
            pltpu.VMEM((2, 2 * LAT, LAT), BF16),
            pltpu.VMEM(gains.shape, F32),
        ),
        in_specs=[hbm] * 12,
        out_specs=(vmem,) * 9,
        scratch_shapes=held
        + [
            pltpu.VMEM((LAT, nodes + slots * SLOT), BF16),
            pltpu.VMEM((2 * LAT, nodes), F32),
            pltpu.VMEM((HALF, max(lane_tiles, 1) * LAT), I32),
            pltpu.VMEM((HALF, nodes), I32),
            pltpu.VMEM((edge_blocks, LAT, group_edges), F32),
            pltpu.VMEM((edge_blocks, LAT, group_edges), BF16),
            pltpu.VMEM((slots, LAT, SLOT), BF16),
            pltpu.VMEM((slots, LAT, SLOT), BF16),
            pltpu.VMEM((2 * TILE, LAT), BF16),
            pltpu.VMEM((nodes, TILE), BF16),
            pltpu.VMEM((nodes, 2 * BORDER), BF16),
            pltpu.VMEM((2 * TILE, nodes), BF16),
            pltpu.VMEM((nodes, LAT), F32),
            pltpu.VMEM((2, 2 * BORDER, LAT), BF16),
            pltpu.VMEM((2, 2 * BORDER, LAT), BF16),
            pltpu.VMEM((EDGE_ROWS, LAT), F32),
            pltpu.VMEM((nodes, 2 * LAT), BF16),
            pltpu.VMEM((groups * LAT, TILE), F32),
            pltpu.VMEM((2 * LAT, LAT), BF16),
            pltpu.VMEM((LAT, 2 * LAT), BF16),
            pltpu.VMEM((LAT, LAT), F32),
            pltpu.VMEM((LAT, LAT), F32),
            pltpu.SemaphoreType.DMA((12,)),
            pltpu.SemaphoreType.DMA((7,)),
            pltpu.SemaphoreType.DMA((7,)),
        ],
        compiler_params=pltpu.CompilerParams(
            collective_id=0, has_side_effects=True, vmem_limit_bytes=64_600_000
        ),
        name="graph_step",
    )(*arrays)
    return pl.pallas_call(
        finish,
        out_shape=(
            jax.ShapeDtypeStruct(fine_nodes.shape, BF16),
            jax.ShapeDtypeStruct(coarse_nodes.shape, BF16),
        ),
        in_specs=[vmem] * 9,
        out_specs=(hbm, hbm),
        scratch_shapes=[
            pltpu.VMEM(fine_nodes.shape, BF16),
            pltpu.VMEM(coarse_nodes.shape, BF16),
            pltpu.SemaphoreType.DMA((groups + 1,)),
        ],
        compiler_params=pltpu.CompilerParams(vmem_limit_bytes=16 * 1024 * 1024),
        name="graph_finish",
    )(*state)


def solution(mesh):
    both = ("region", "level")
    in_specs = (
        P(both, None),
        P(both, None),
        P(both, None),
        P(both),
        P(both),
        P(both),
        P(both),
        P(both),
        P(),
        P(),
        P(),
        P(),
    )
    return jax.shard_map(
        functools.partial(body, mesh.shape["level"]),
        mesh=mesh,
        in_specs=in_specs,
        out_specs=(P(both, None), P(both, None)),
        check_vma=False,
    )
```
